32 devices in a mesh: rep: 2 (over y), ep: 16 (over z, x, core).
Axes of the slice: x: 2, y: 2, z: 4, core: 2. Of those that a mesh axis runs over, the one named last changes fastest.
Arguments:
- tokens: bfloat16 [512, 2048], P(('rep', 'ep')), may hold values from -6 to 6
- logits: float32 [512, 8], P(('rep', 'ep')), may hold values from -6 to 6
- expert_ids: int32 [512, 8], P(('rep', 'ep')), may hold values from 0 to 15, all different within a row; in each aligned block of 16 rows (0 to 15, 16 to 31, ...) at most 16 rows name the same one
- w_gate_up: bfloat16 [16, 2, 2048, 1536], P('ep', None, None, 'rep'), may hold values from -0.125 to 0.125
- w_down: bfloat16 [16, 1536, 2048], P('ep', None, 'rep'), may hold values from -0.15625 to 0.15625
Outputs:
- mixed: bfloat16 [512, 2048], P(('rep', 'ep'))
The draws below stay inside these ranges and needn't reach their ends.
Inputs may be any that keep to these rules, and one draw needn't show every extreme that they name: `expert_ids`: each token names 8 different experts; the 16 tokens of one device name any one expert at most 16 times.
All inputs are finite; a program needn't handle non-finite values.
Results may differ from the reference program's by a relative error of at most 0.0057.
Values may be sent and summed in bfloat16 or wider, within the bound.
A program may use at most 64 MiB of HBM per device.

```python
import math
import jax
import jax.numpy as jnp
import numpy as np
from jax import lax

D = 2048
H = 1536
TOPK = 8
TOK_DEV = 16
E = 16
MOST = 16
TOKENS = 512
N_REP = 2
N_EP = 16


def steps_of(own_key, extent, cuts, least, top_value):
    loudness = 1.0
    for dim, blocks in cuts:
        draws = jax.random.uniform(jax.random.fold_in(jax.random.fold_in(own_key, 6), dim), (blocks,), jnp.float32, least / len(cuts), top_value / len(cuts))
        loudness = loudness * jnp.repeat(jnp.exp(draws), extent[dim] // blocks).reshape((-1,) + (1,) * (len(extent) - 1 - dim))
    return loudness


def deal_out(stream_key, own, number, rows, amount, top, limit, lean):
    ranking = jax.random.permutation(stream_key, amount)
    heavy_load, ordinary = load_shares(amount, rows * top, limit, lean, True), load_shares(amount, rows * top, limit, lean, False)
    places = jnp.arange(amount)

    def named(sizes, turn):
        used = int((sizes > 0).sum())
        fixed = max(1, used // 4)
        passed = fixed + (places - fixed + turn * (used - fixed)) % max(1, amount - fixed)
        return jnp.zeros((amount,), jnp.int32).at[ranking[jnp.where(places < fixed, places, passed)]].set(jnp.asarray(sizes, jnp.int32))

    sizes = jnp.where(number % 4 == 0, named(heavy_load, number // 4), named(ordinary, number - number // 4 - 1))
    mixed = jax.random.permutation(jax.random.fold_in(own, 3), amount)
    giver, receiver = mixed[0:amount // 2 * 2:2], mixed[1:amount // 2 * 2:2]
    room = jnp.minimum(sizes[giver] - 1, limit - sizes[receiver]) // 2
    room = jnp.where((giver == ranking[0]) | (receiver == ranking[0]) | (sizes[receiver] == 0), 0, jnp.maximum(room, 0))
    passed = jax.random.randint(jax.random.fold_in(own, 4), (amount // 2,), 0, 1 << 20) % (room + 1)
    sizes = sizes.at[giver].add(-passed).at[receiver].add(passed)
    items = jnp.searchsorted(jnp.cumsum(sizes), jnp.arange(rows * top), side="right").astype(jnp.int32)
    listing = items.reshape(top, rows).T
    listing = listing[jax.random.permutation(jax.random.fold_in(own, 1), rows)]
    turn = jax.random.randint(jax.random.fold_in(own, 2), (rows, 1), 0, top)
    return jnp.take_along_axis(listing, (jnp.arange(top)[None, :] + turn) % top, axis=1)


def load_shares(number_of, total, most, skew, full):
    portions = [(1 << 20) // math.isqrt(standing ** skew) + 1 for standing in range(1, number_of + 1)]
    largest = most if full else min(most, max(-(-total // number_of), total * portions[0] // sum(portions)))
    least = 1 if total - largest >= number_of - 1 else 0
    given, rest = [largest] + [least] * (number_of - 1), total - largest - least * (number_of - 1)
    while rest > 0:
        candidates = [i for i in range(1, number_of) if given[i] < largest] or [i for i in range(1, number_of) if given[i] < most]
        mass, remaining = sum([portions[i] for i in candidates]), rest
        for i in candidates:
            extra = min(most - given[i], max(1, remaining * portions[i] // mass), rest)
            given[i] = given[i] + extra
            rest = rest - extra
    return np.array(given)


def centred(stream_key, extent, deviation, limit, shards=(), kind=jnp.bfloat16):
    drawn = deviation * jax.random.normal(stream_key, extent, jnp.float32)
    if shards:
        drawn = drawn * steps_of(stream_key, extent, shards, -0.22, 0.18)
    return jnp.clip(drawn, -limit, limit).astype(kind)


def setup_inputs(seed: int = 0) -> dict:
    keys = jax.random.split(jax.random.key(seed), 6)
    tokens = centred(keys[0], (TOKENS, D), 1.0, 6.0, ((0, 32),))
    logits = centred(keys[1], (TOKENS, TOPK), 1.5, 6.0, ((0, 32),), jnp.float32)
    expert_ids_keys = jax.random.split(jax.random.fold_in(keys[2], 1), TOKENS // TOK_DEV)
    expert_ids_turns = jax.random.permutation(jax.random.fold_in(keys[2], 3), TOKENS // TOK_DEV)
    expert_ids = jax.vmap(lambda own, number: deal_out(jax.random.fold_in(keys[2], 2), own, number, TOK_DEV, E, TOPK, MOST, 2))(expert_ids_keys, expert_ids_turns).reshape((TOKENS, TOPK))
    w_gate_up = centred(keys[3], (E, 2, D, H), D ** -0.5, 0.125, ((0, 16), (3, 2)))
    w_down = centred(keys[4], (E, H, D), H ** -0.5, 0.15625, ((0, 16), (2, 2)))
    return dict(tokens=tokens, logits=logits, expert_ids=expert_ids, w_gate_up=w_gate_up, w_down=w_down)


def reference(tokens, logits, expert_ids, w_gate_up, w_down):
    slot_total = TOKENS * TOPK
    block_size = N_REP * N_EP * MOST
    flat_ids = expert_ids.reshape(slot_total).astype(jnp.int32)
    ordering = jnp.argsort(flat_ids, stable=True).astype(jnp.int32)
    experts = jnp.arange(E, dtype=jnp.int32)
    counts = jnp.sum((flat_ids[None, :] == experts[:, None]).astype(jnp.int32), axis=1).astype(jnp.int32)
    starts = (jnp.cumsum(counts) - counts).astype(jnp.int32)
    padded = jnp.concatenate([ordering, jnp.full((block_size,), slot_total, jnp.int32)])

    def expert_rows(triple):
        expert, start, count = triple
        picked = lax.dynamic_slice_in_dim(padded, start, block_size)
        usable = jnp.arange(block_size, dtype=jnp.int32) < count
        source = jnp.minimum(picked, slot_total - 1) // TOPK
        slot_rows = tokens[source].astype(jnp.float32)
        gate_part = jnp.dot(slot_rows, w_gate_up[expert, 0].astype(jnp.float32))
        upper = jnp.dot(slot_rows, w_gate_up[expert, 1].astype(jnp.float32))
        hidden = (jax.nn.silu(gate_part) * upper).astype(jnp.bfloat16)
        output = jnp.dot(hidden.astype(jnp.float32), w_down[expert].astype(jnp.float32)).astype(jnp.bfloat16)
        targets = jnp.where(usable, picked, slot_total).astype(jnp.int32)
        return output, targets

    outputs, targets = lax.map(expert_rows, (experts, starts, counts))
    gathered = jnp.zeros((slot_total + 1, D), jnp.bfloat16).at[targets.reshape(-1)].set(outputs.reshape(-1, D))
    per_slot = gathered[:slot_total].reshape(TOKENS, TOPK, D).astype(jnp.float32)
    scaled = jnp.exp(logits)
    weights = scaled / jnp.sum(scaled, axis=1, keepdims=True)
    mixed = jnp.sum(weights[:, :, None] * per_slot, axis=1)
    return mixed.astype(jnp.bfloat16)
```

```python
import functools

import jax
import jax.numpy as jnp
from jax import lax
from jax.experimental import pallas as pl
from jax.experimental.pallas import tpu as pltpu
from jax.sharding import PartitionSpec as P


def slot_plan(choice_ids, expert_count, capacity):
    queue_len, picks = choice_ids.shape
    flat_ids = choice_ids.reshape(queue_len * picks)
    position = jnp.arange(queue_len * picks, dtype=jnp.int32)
    earlier = (flat_ids[:, None] == flat_ids[None, :]) & (position[None, :] < position[:, None])
    slot_rank = jnp.sum(earlier.astype(jnp.int32), axis=1)
    target = flat_ids * capacity + slot_rank
    columns = jnp.arange(expert_count * capacity, dtype=jnp.int32)
    onehot = target[:, None] == columns[None, :]
    return onehot.reshape(queue_len, picks, expert_count * capacity)


def dispatch_rows(onehot, tokens):
    placing = jnp.sum(onehot.astype(jnp.bfloat16), axis=1)
    return jnp.dot(placing.T, tokens, preferred_element_type=jnp.float32).astype(jnp.bfloat16)


def to_owners(outgoing):
    return lax.all_to_all(outgoing, "ep", split_axis=0, concat_axis=0, tiled=True)


def to_sources(results):
    return lax.all_to_all(results, "ep", split_axis=0, concat_axis=0, tiled=True)


def full_units(quarter):
    return lax.all_gather(quarter, "rep", axis=1, tiled=True)


MESH = pl.DeviceIdType.MESH
PAD = 128


TILE = 256


def hidden_passes(nz):
    passes = [
        [(0, 0, 0)],
        [(0, 0, 1), (1, 0, 0), (0, 1, 0)],
        [(1, 0, 1), (0, 1, 1), (1, 1, 0)],
        [(1, 1, 1), (2, 0, 0), (2, 0, 1), (2, 1, 0)],
        [(2, 1, 1), (3, 0, 0), (3, 0, 1)],
        [(3, 1, 0), (3, 1, 1)],
    ]
    passes = [[chip for chip in chips if chip[0] < nz] for chips in passes]
    return [chips for chips in passes if chips]


def dense_kernel(nz, tok_ref, logit_ref, ids_ref, wgu_ref, wd_ref, out_ref,
                 rows, logit_v, ids_v, gate_w, up_w, down_w, hid, own, core_in, pair, keep, x_in,
                 part, z_in, cross, y_in,
                 w_sem, near_send, line_send, far_recv, pass_recv, hid_send, hid_recv, core_send, core_recv,
                 x_send, x_recv, z_send, z_recv, y_send, y_recv):
    y = lax.axis_index("rep")
    ep = lax.axis_index("ep")
    z, x, c = ep // 4, (ep // 2) % 2, ep % 2
    oy, ox, oc = 1 - y, 1 - x, 1 - c
    q, width = tok_ref.shape
    units = gate_w.shape[1]
    cols = down_w.shape[1]
    n_ep = 4 * nz
    tiles = units // TILE

    def at(yy, zz, xx, cc):
        return (yy, zz * 4 + xx * 2 + cc)

    small = [
        pltpu.make_async_copy(logit_ref, logit_v, w_sem.at[0]),
        pltpu.make_async_copy(ids_ref, ids_v, w_sem.at[1]),
        pltpu.make_async_copy(tok_ref, rows.at[z, x, y, c, :, pl.ds(0, width)], w_sem.at[2]),
    ]
    weights = [
        pltpu.make_async_copy(wgu_ref.at[0, 0], gate_w, w_sem.at[3]),
        pltpu.make_async_copy(wgu_ref.at[0, 1], up_w, w_sem.at[4]),
        pltpu.make_async_copy(wd_ref.at[0], down_w, w_sem.at[5]),
    ]
    for w in small + weights:
        w.start()

    barrier = pltpu.get_barrier_semaphore()
    peers = [at(oy, z, x, c), at(y, z, ox, c), at(y, z, x, oc), at(oy, z, ox, c)]
    peers += [at(y, (z + d) % nz, x, c) for d in range(1, nz)]
    for p in peers:
        pl.semaphore_signal(barrier, inc=1, device_id=p, device_id_type=MESH)

    for w in small:
        w.wait()
    scaled = jnp.exp(logit_v[...])
    soft = scaled / jnp.sum(scaled, axis=0, keepdims=True)
    line = lax.broadcasted_iota(jnp.int32, (PAD, q), 0)
    expert, piece = line % n_ep, line // n_ep
    ids = ids_v[...]
    comb = jnp.zeros((PAD, q), jnp.float32)
    for k in range(ids.shape[0]):
        comb = comb + jnp.where(ids[k:k + 1, :] == expert, soft[k:k + 1, :], 0.0)
    hi = comb.astype(jnp.bfloat16).astype(jnp.float32)
    rest = comb - hi
    mid = rest.astype(jnp.bfloat16).astype(jnp.float32)
    low = rest - mid
    coded = jnp.where(piece == 0, hi, jnp.where(piece == 1, mid, jnp.where(piece == 2, low, 0.0)))
    rows[z, x, y, c, :, width:] = coded.T.astype(jnp.bfloat16)
    with jax.named_scope("entry"):
        pl.semaphore_wait(barrier, len(peers))

    near = jnp.minimum(z, nz - 1 - z)
    rising = z < nz - 1 - z
    order = [z]
    for k in range(1, nz):
        d = jnp.where(k <= 2 * near, (k + 1) // 2, k - near)
        sign = jnp.where(k <= 2 * near, -1 if k % 2 else 1, jnp.where(rising, 1, -1))
        order.append(z + sign * d)
    up, down = at(y, jnp.minimum(z + 1, nz - 1), x, c), at(y, jnp.maximum(z - 1, 0), x, c)

    passes = hidden_passes(nz)
    pass_of = {chip: number for number, chips in enumerate(passes) for chip in chips}

    def place(chip):
        k, dx, dy = chip
        return order[k], (x, ox)[dx], (y, oy)[dy]

    def send(dev, chip, send_sem, recv_sem):
        block = rows.at[(*place(chip), c)]
        pltpu.make_async_remote_copy(
            src_ref=block, dst_ref=block, send_sem=send_sem, recv_sem=recv_sem,
            device_id=dev, device_id_type=MESH).start()

    def far_sem(s):
        return far_recv.at[(s[0] * 2 + s[1]) * 2 + s[2]]

    def wait_blocks(ref, send_sem=None, recv_sem=None):
        copy = pltpu.make_async_remote_copy(
            src_ref=ref, dst_ref=ref, send_sem=send_sem if recv_sem is None else recv_sem,
            recv_sem=send_sem if recv_sem is None else recv_sem,
            device_id=peers[0], device_id_type=MESH)
        if recv_sem is None:
            copy.wait_send()
        else:
            copy.wait_recv()

    def arrive(chip):
        wait_blocks(rows.at[(*place(chip), c)], recv_sem=far_sem(place(chip)))

    def arrive_pass(number):
        count = len(passes[number])
        if count == 1:
            ref = rows.at[0, 0, 0, 0]
        elif count == 2:
            ref = rows.at[0, 0, 0]
        elif count == 3:
            ref = rows.at[0, 0].reshape(4, q, width + PAD).at[pl.ds(0, 3)]
        else:
            ref = rows.at[0, 0]
        wait_blocks(ref, recv_sem=pass_recv.at[number])

    def send_z(chip):
        k, s = chip[0], place(chip)
        if k:
            go_up = jnp.logical_and(order[k] < z, z < nz - 1)
            go_down = jnp.logical_and(order[k] > z, z > 0)
        else:
            go_up, go_down = z < nz - 1, z > 0

        @pl.when(go_up)
        def _():
            send(up, chip, line_send.at[k], far_sem(s))

        @pl.when(go_down)
        def _():
            send(down, chip, line_send.at[k if k else nz], far_sem(s))

    def settle_z(k):
        def wait(sem):
            wait_blocks(rows.at[0, 0, 0], send_sem=sem)
        if k:
            go = jnp.logical_or(
                jnp.logical_and(order[k] < z, z < nz - 1), jnp.logical_and(order[k] > z, z > 0))
            pl.when(go)(lambda: wait(line_send.at[k]))
        else:
            pl.when(z < nz - 1)(lambda: wait(line_send.at[0]))
            pl.when(z > 0)(lambda: wait(line_send.at[nz]))

    def send_x(chip):
        send(peers[1], chip, near_send.at[1], far_sem(place(chip)))

    def send_core(chip):
        send(peers[2], chip, near_send.at[2], pass_recv.at[pass_of[chip]])

    def forward(chip):
        k, dx, dy = chip
        with jax.named_scope(f"fw{k}{dx}{dy}"):
            arrive(chip)
        if dx == 0:
            if k:
                send_x(chip)
            send_z(chip)
        send_core(chip)

    def hid_copy(chip, at_cols):
        k, dx = chip[:2]
        part_of = hid.at[y, k, dx, (y, oy)[chip[2]], :, at_cols]
        return pltpu.make_async_remote_copy(
            src_ref=part_of, dst_ref=part_of,
            send_sem=hid_send, recv_sem=hid_recv.at[k, dx],
            device_id=peers[0], device_id_type=MESH)

    def hidden_of(number, chips):
        with jax.named_scope(f"rows{number}"):
            arrive_pass(number)
        with jax.named_scope(f"hidden{number}"):
            block = jnp.concatenate([rows[(*place(chip),)].reshape(2 * q, width + PAD)[:, :width] for chip in chips], axis=0)
            for i in range(tiles):
                at_cols = pl.ds(i * TILE, TILE)
                gate = jnp.dot(block, gate_w[:, at_cols], preferred_element_type=jnp.float32)
                upper = jnp.dot(block, up_w[:, at_cols], preferred_element_type=jnp.float32)
                value = (jax.nn.silu(gate) * upper).astype(jnp.bfloat16)
                for j, chip in enumerate(chips):
                    yy = (y, oy)[chip[2]]
                    hid[y, chip[0], chip[1], yy, :, at_cols] = value[j * 2 * q:(j + 1) * 2 * q]
                    if number == 0:
                        hid_copy(chip, at_cols).start()
                    elif i == tiles - 1:
                        hid_copy(chip, pl.ds(0, units)).start()

    def core_copy(k, dx):
        return pltpu.make_async_remote_copy(
            src_ref=own.at[k, dx, oc], dst_ref=core_in.at[k, dx],
            send_sem=core_send, recv_sem=core_recv.at[k, dx],
            device_id=peers[2], device_id_type=MESH)

    def x_copy(k):
        return pltpu.make_async_remote_copy(
            src_ref=pair.at[k], dst_ref=x_in.at[k],
            send_sem=x_send, recv_sem=x_recv.at[k],
            device_id=peers[1], device_id_type=MESH)

    def z_copy(k, slot):
        return pltpu.make_async_remote_copy(
            src_ref=part.at[k], dst_ref=z_in.at[slot],
            send_sem=z_send, recv_sem=z_recv.at[slot],
            device_id=at(y, order[k], x, c), device_id_type=MESH)

    def outputs_of(*groups):
        size = 4 * q
        name = "".join(f"{k}{dx}" for k, dx in groups)
        with jax.named_scope(f"hid{name}"):
            for k, dx in groups:
                wait_blocks(hid.at[oy, k, dx], recv_sem=hid_recv.at[k, dx])
        with jax.named_scope(f"out{name}"):
            picked = lax.broadcasted_iota(jnp.int32, (size, PAD), 1)
            take = jnp.logical_and(picked % n_ep == ep, picked < 3 * n_ep)
            weights, halves = [], ([], [])
            for k, dx in groups:
                codes = rows[order[k], (x, ox)[dx]].reshape(size, width + PAD)[:, width:].astype(jnp.float32)
                weights.append(jnp.sum(jnp.where(take, codes, 0.0), axis=1, keepdims=True))
                for half in range(2):
                    halves[half].append(hid[half, k, dx].reshape(size, units))
            left, right = jnp.concatenate(halves[0], axis=0), jnp.concatenate(halves[1], axis=0)
            for i in range(cols // TILE):
                at_cols = pl.ds(i * TILE, TILE)
                total = jnp.dot(left, down_w[:units, at_cols], preferred_element_type=jnp.float32)
                total += jnp.dot(right, down_w[units:, at_cols], preferred_element_type=jnp.float32)
                total = total.astype(jnp.bfloat16).astype(jnp.float32)
                for j, (k, dx) in enumerate(groups):
                    value = (total[j * size:(j + 1) * size] * weights[j]).astype(jnp.bfloat16).reshape(2, 2, q, TILE)
                    own[k, dx, 0, :, :, at_cols] = value[:, 0]
                    own[k, dx, 1, :, :, at_cols] = value[:, 1]
        for k, dx in groups:
            core_copy(k, dx).start()

    def over_core(k, dx):
        with jax.named_scope(f"core{k}{dx}"):
            core_copy(k, dx).wait_recv()
        both = own[k, dx, c].astype(jnp.float32) + core_in[k, dx].astype(jnp.float32)
        if dx:
            pair[k] = both.astype(jnp.bfloat16)
            x_copy(k).start()
        else:
            keep[k] = both

    def over_x(k):
        with jax.named_scope(f"x{k}"):
            x_copy(k).wait_recv()
        total = keep[k] + x_in[k].astype(jnp.float32)
        if k:
            part[k] = total.astype(jnp.bfloat16)
            z_copy(k, z).start()
        else:
            keep[k] = total

    mine = (0, 0, 0)
    send(peers[0], mine, near_send.at[0], far_sem(place(mine)))
    send_core(mine)
    send_z(mine)
    send_x(mine)
    for w in weights[:2]:
        w.wait()
    if nz == 4:
        hidden_of(0, passes[0])
        send(peers[3], mine, near_send.at[3], far_sem(place(mine)))
        for chip in [(0, 0, 1), (1, 0, 0), (0, 1, 0)]:
            forward(chip)
        hidden_of(1, passes[1])
        for chip in [(1, 0, 1), (2, 0, 0), (0, 1, 1), (1, 1, 0)]:
            forward(chip)
        hidden_of(2, passes[2])
        weights[2].wait()
        for chip in [(2, 0, 1), (1, 1, 1)]:
            forward(chip)
        outputs_of((0, 0))
        for chip in [(2, 1, 0), (3, 0, 0)]:
            forward(chip)
        hidden_of(3, passes[3])
        over_core(0, 0)
        for chip in [(3, 0, 1), (2, 1, 1)]:
            forward(chip)
        hidden_of(4, passes[4])
        outputs_of((0, 1), (1, 0))
        forward((3, 1, 0))
        over_core(0, 1)
        over_core(1, 0)
        forward((3, 1, 1))
        hidden_of(5, passes[5])
        outputs_of((1, 1), (2, 0))
        over_core(1, 1)
        over_core(2, 0)
        outputs_of((2, 1), (3, 0))
        over_x(0)
        over_x(1)
        over_core(2, 1)
        over_core(3, 0)
        outputs_of((3, 1))
        over_core(3, 1)
        over_x(2)
        over_x(3)
    else:
        send(peers[3], mine, near_send.at[3], far_sem(place(mine)))
        for number, chips in enumerate(passes):
            for chip in chips:
                if chip != mine:
                    forward(chip)
            hidden_of(number, chips)
        weights[2].wait()
        for k in [*range(1, nz), 0]:
            for dx in range(2):
                outputs_of((k, dx))
                over_core(k, dx)
        for k in range(nz):
            over_x(k)

    total = keep[0]
    for k in range(1, nz):
        with jax.named_scope(f"z{k}"):
            z_copy(k, order[k]).wait_recv()
        total = total + z_in[order[k]].astype(jnp.float32)
    cross[...] = total.astype(jnp.bfloat16)
    y_copy = pltpu.make_async_remote_copy(
        src_ref=cross.at[oy], dst_ref=y_in, send_sem=y_send, recv_sem=y_recv,
        device_id=peers[0], device_id_type=MESH)
    y_copy.start()
    out_ref[:, pl.ds(pl.multiple_of(y * cols, cols), cols)] = cross[y]

    one = rows.at[0, 0, 0, 0]
    wait_blocks(one, send_sem=near_send.at[0])
    wait_blocks(one, send_sem=near_send.at[3])
    wait_blocks(rows.at[0, 0].reshape(4, q, width + PAD).at[pl.ds(0, 1)] if nz < 2 else rows.at[0, :, :, :].reshape(8, q, width + PAD).at[pl.ds(0, 2 * nz - 1)], send_sem=near_send.at[1])
    wait_blocks(rows.reshape(8 * nz, q, width + PAD).at[pl.ds(0, 4 * nz)], send_sem=near_send.at[2])
    for k in range(nz):
        settle_z(k)
    wait_blocks(hid.at[y], send_sem=hid_send)
    wait_blocks(own.reshape(nz * 4, 2, q, cols).at[pl.ds(0, 2 * nz)], send_sem=core_send)
    wait_blocks(pair, send_sem=x_send)
    if nz > 1:
        wait_blocks(part.at[pl.ds(1, nz - 1)], send_sem=z_send)
    with jax.named_scope("last"):
        y_copy.wait_send()
        y_copy.wait_recv()
    out_ref[:, pl.ds(pl.multiple_of(oy * cols, cols), cols)] = y_in[...]


def dense_body(tokens, logits, expert_ids, w_gate_up, w_down):
    nz = lax.axis_size("ep") // 4
    q, width = tokens.shape
    picks = logits.shape[1]
    units = w_gate_up.shape[3]
    cols = w_down.shape[2]
    bf, sem = jnp.bfloat16, pltpu.SemaphoreType.DMA
    vmem = pl.BlockSpec(memory_space=pltpu.VMEM)
    hbm = pl.BlockSpec(memory_space=pl.ANY)
    return pl.pallas_call(
        functools.partial(dense_kernel, nz),
        out_shape=pltpu.VMEM((q, width), bf),
        in_specs=[hbm] * 5,
        out_specs=vmem,
        scratch_shapes=[
            pltpu.VMEM((nz, 2, 2, 2, q, width + PAD), bf),
            pltpu.VMEM((picks, q), jnp.float32),
            pltpu.VMEM((picks, q), jnp.int32),
            pltpu.VMEM((width, units), bf),
            pltpu.VMEM((width, units), bf),
            pltpu.VMEM((2 * units, cols), bf),
            pltpu.VMEM((2, nz, 2, 2, 2 * q, units), bf),
            pltpu.VMEM((nz, 2, 2, 2, q, cols), bf),
            pltpu.VMEM((nz, 2, 2, q, cols), bf),
            pltpu.VMEM((nz, 2, q, cols), bf),
            pltpu.VMEM((nz, 2, q, cols), jnp.float32),
            pltpu.VMEM((nz, 2, q, cols), bf),
            pltpu.VMEM((nz, 2, q, cols), bf),
            pltpu.VMEM((nz, 2, q, cols), bf),
            pltpu.VMEM((2, q, cols), bf),
            pltpu.VMEM((q, cols), bf),
            sem((6,)),
            sem((4,)), sem((nz + 1,)), sem((4 * nz,)), sem((6,)),
            sem, sem((nz, 2)),
            sem, sem((nz, 2)),
            sem, sem((nz,)),
            sem, sem((nz,)),
            sem, sem,
        ],
        compiler_params=pltpu.CompilerParams(
            collective_id=0, has_side_effects=True, vmem_limit_bytes=58 * 1024 * 1024
        ),
    )(tokens, logits.T, expert_ids.T, w_gate_up, w_down)


def body(tokens, logits, expert_ids, w_gate_up, w_down):
    expert_count = lax.axis_size("ep")
    queue_len, picks = expert_ids.shape
    features = tokens.shape[1]
    capacity = max(2, min(queue_len, 2 * queue_len * picks // expert_count))
    if capacity == queue_len and lax.axis_size("rep") == 2 and expert_count % 8 == 0 and 3 * expert_count <= PAD:
        return dense_body(tokens, logits, expert_ids, w_gate_up, w_down)
    slot_total = expert_count * capacity
    onehot = slot_plan(expert_ids, expert_count, capacity)
    scaled = jnp.exp(logits)
    weights = scaled / jnp.sum(scaled, axis=1, keepdims=True)
    combine = jnp.sum(weights[:, :, None] * onehot.astype(jnp.float32), axis=1)
    gate_weight = w_gate_up[0, 0]
    up_weight = w_gate_up[0, 1]
    down_weight = w_down[0]
    received = to_owners(dispatch_rows(onehot, tokens).reshape(expert_count, capacity, features))
    slot_rows = received.reshape(slot_total, features)
    portion = lax.all_gather(slot_rows, "rep", axis=0, tiled=True)
    gate_part = jnp.dot(portion, gate_weight, preferred_element_type=jnp.float32)
    upper = jnp.dot(portion, up_weight, preferred_element_type=jnp.float32)
    quarter = (jax.nn.silu(gate_part) * upper).astype(jnp.bfloat16)
    hidden = full_units(quarter)
    partial_out = jnp.dot(hidden, down_weight, preferred_element_type=jnp.float32).astype(
        jnp.bfloat16
    )
    own_rows = lax.all_to_all(partial_out, "rep", split_axis=0, concat_axis=1, tiled=True)
    returned = to_sources(own_rows.reshape(expert_count, capacity, features))
    values = returned.reshape(slot_total, features)
    mixed = jnp.dot(combine, values.astype(jnp.float32), precision=lax.Precision.HIGHEST)
    return mixed.astype(jnp.bfloat16)


def solution(mesh):
    in_specs = (
        P(("rep", "ep"), None),
        P(("rep", "ep"), None),
        P(("rep", "ep"), None),
        P("ep", None, None, "rep"),
        P("ep", None, "rep"),
    )
    out_specs = P(("rep", "ep"), None)
    return jax.shard_map(body, mesh=mesh, in_specs=in_specs, out_specs=out_specs, check_vma=False)
```

```python
import jax
import jax.numpy as jnp
from jax import lax
from jax.experimental import pallas as pl
from jax.experimental.pallas import tpu as pltpu
from jax.sharding import PartitionSpec as P


def slot_plan(choice_ids, expert_count, capacity):
    queue_len, picks = choice_ids.shape
    flat_ids = choice_ids.reshape(queue_len * picks)
    position = jnp.arange(queue_len * picks, dtype=jnp.int32)
    earlier = (flat_ids[:, None] == flat_ids[None, :]) & (position[None, :] < position[:, None])
    slot_rank = jnp.sum(earlier.astype(jnp.int32), axis=1)
    target = flat_ids * capacity + slot_rank
    columns = jnp.arange(expert_count * capacity, dtype=jnp.int32)
    onehot = target[:, None] == columns[None, :]
    return onehot.reshape(queue_len, picks, expert_count * capacity)


def dispatch_rows(onehot, tokens):
    placing = jnp.sum(onehot.astype(jnp.bfloat16), axis=1)
    return jnp.dot(placing.T, tokens, preferred_element_type=jnp.float32).astype(jnp.bfloat16)


def to_owners(outgoing):
    return lax.all_to_all(outgoing, "ep", split_axis=0, concat_axis=0, tiled=True)


def to_sources(results):
    return lax.all_to_all(results, "ep", split_axis=0, concat_axis=0, tiled=True)


def full_units(quarter):
    return lax.all_gather(quarter, "rep", axis=1, tiled=True)


MESH = pl.DeviceIdType.MESH
PAD = 128


TILE = 256


NZ = 4
PASSES = [
    [(0, 0, 0)],
    [(1, 0, 0), (0, 1, 0)],
    [(1, 1, 0), (1, 0, 1), (2, 0, 0), (3, 0, 0)],
    [(1, 1, 1), (3, 1, 0), (3, 0, 1), (2, 0, 1)],
    [(2, 1, 0), (3, 1, 1)],
    [(2, 1, 1)],
    [(0, 0, 1), (0, 1, 1)],
]


def dense_kernel(tok_ref, logit_ref, ids_ref, wgu_ref, wd_ref, out_ref,
                 rows, logit_v, ids_v, gate_w, up_w, down_w, hid, own, core_in, pair, keep, x_in,
                 part, z_in, zy_in, cross, y_in, x0_in, xy_in,
                 w_sem, near_send, line_send, far_recv, pass_recv, hid_send, hid_recv, core_send, core_recv,
                 x_send, x_recv, z_send, z_recv, zy_recv, y_send, y_recv, xy_recv):
    y = lax.axis_index("rep")
    ep = lax.axis_index("ep")
    z, x, c = ep // 4, (ep // 2) % 2, ep % 2
    oy, ox, oc = 1 - y, 1 - x, 1 - c
    q, width = tok_ref.shape
    units = gate_w.shape[1]
    cols = down_w.shape[1]
    nz, n_ep = NZ, 4 * NZ
    tiles = units // TILE

    def at(yy, zz, xx, cc):
        return (yy, zz * 4 + xx * 2 + cc)

    small = [
        pltpu.make_async_copy(logit_ref, logit_v, w_sem.at[0]),
        pltpu.make_async_copy(ids_ref, ids_v, w_sem.at[1]),
        pltpu.make_async_copy(tok_ref, rows.at[z, x, y, c, :, pl.ds(0, width)], w_sem.at[2]),
    ]
    weights = [
        pltpu.make_async_copy(wgu_ref.at[0, 0], gate_w, w_sem.at[3]),
        pltpu.make_async_copy(wgu_ref.at[0, 1], up_w, w_sem.at[4]),
        pltpu.make_async_copy(wd_ref.at[0], down_w, w_sem.at[5]),
    ]
    for w in small + weights:
        w.start()

    barrier = pltpu.get_barrier_semaphore()
    peers = [at(oy, z, x, c), at(y, z, ox, c), at(y, z, x, oc)]
    peers += [at(yy, (z + d) % nz, x, c) for yy in (y, oy) for d in range(1, nz)]
    peers += [at(oy, z, ox, c)]
    for p in peers:
        pl.semaphore_signal(barrier, inc=1, device_id=p, device_id_type=MESH)

    for w in small:
        w.wait()
    scaled = jnp.exp(logit_v[...])
    soft = scaled / jnp.sum(scaled, axis=0, keepdims=True)
    line = lax.broadcasted_iota(jnp.int32, (PAD, q), 0)
    expert, piece = line % n_ep, line // n_ep
    ids = ids_v[...]
    comb = jnp.zeros((PAD, q), jnp.float32)
    for k in range(ids.shape[0]):
        comb = comb + jnp.where(ids[k:k + 1, :] == expert, soft[k:k + 1, :], 0.0)
    hi = comb.astype(jnp.bfloat16).astype(jnp.float32)
    rest = comb - hi
    mid = rest.astype(jnp.bfloat16).astype(jnp.float32)
    low = rest - mid
    coded = jnp.where(piece == 0, hi, jnp.where(piece == 1, mid, jnp.where(piece == 2, low, 0.0)))
    rows[z, x, y, c, :, width:] = coded.T.astype(jnp.bfloat16)
    with jax.named_scope("entry"):
        pl.semaphore_wait(barrier, len(peers))

    near = jnp.minimum(z, nz - 1 - z)
    rising = z < nz - 1 - z
    order = [z]
    for k in range(1, nz):
        d = jnp.where(k <= 2 * near, (k + 1) // 2, k - near)
        sign = jnp.where(k <= 2 * near, -1 if k % 2 else 1, jnp.where(rising, 1, -1))
        order.append(z + sign * d)
    up, down = at(y, jnp.minimum(z + 1, nz - 1), x, c), at(y, jnp.maximum(z - 1, 0), x, c)

    chain = [[(z < nz - 1, up, 1), (z > 0, down, 2)], [(z == 2, up, 3)], [(z == 1, down, 3)]]
    pass_of = {chip: number for number, chips in enumerate(PASSES) for chip in chips}

    def place(chip):
        k, dx, dy = chip
        return order[k], (x, ox)[dx], (y, oy)[dy]

    def send(dev, chip, send_sem, recv_sem):
        block = rows.at[(*place(chip), c)]
        pltpu.make_async_remote_copy(
            src_ref=block, dst_ref=block, send_sem=send_sem, recv_sem=recv_sem,
            device_id=dev, device_id_type=MESH).start()

    def far_sem(s):
        return far_recv.at[(s[0] * 2 + s[1]) * 2 + s[2]]

    def wait_blocks(ref, send_sem=None, recv_sem=None):
        copy = pltpu.make_async_remote_copy(
            src_ref=ref, dst_ref=ref, send_sem=send_sem if recv_sem is None else recv_sem,
            recv_sem=send_sem if recv_sem is None else recv_sem,
            device_id=peers[0], device_id_type=MESH)
        if recv_sem is None:
            copy.wait_send()
        else:
            copy.wait_recv()

    def arrive(chip):
        wait_blocks(rows.at[(*place(chip), c)], recv_sem=far_sem(place(chip)))

    def blocks(count):
        return rows.reshape(8 * nz, q, width + PAD).at[pl.ds(0, count)]

    def arrive_pass(number):
        wait_blocks(blocks(len(PASSES[number])), recv_sem=pass_recv.at[number])

    def send_y(chip):
        send(peers[0], chip, near_send.at[0], far_sem(place(chip)))

    def send_x(chip):
        send(peers[1], chip, near_send.at[1], far_sem(place(chip)))

    def send_core(chip):
        send(peers[2], chip, near_send.at[2], pass_recv.at[pass_of[chip]])

    def take(chip):
        k, dx, dy = chip
        with jax.named_scope(f"fw{k}{dx}{dy}"):
            arrive(chip)
        send_core(chip)
        if (dx, dy) == (0, 1) and k < 3:
            for go, dev, sem in chain[k]:
                pl.when(go)(lambda: send(dev, chip, line_send.at[sem], far_sem(place(chip))))

    def hid_copy(chip, at_cols):
        k, dx = chip[:2]
        part_of = hid.at[y, k, dx, (y, oy)[chip[2]], :, at_cols]
        return pltpu.make_async_remote_copy(
            src_ref=part_of, dst_ref=part_of,
            send_sem=hid_send, recv_sem=hid_recv.at[k, dx],
            device_id=peers[0], device_id_type=MESH)

    def hidden_of(number, chips):
        with jax.named_scope(f"rows{number}"):
            arrive_pass(number)
        with jax.named_scope(f"hidden{number}"):
            block = jnp.concatenate([rows[(*place(chip),)].reshape(2 * q, width + PAD)[:, :width] for chip in chips], axis=0)
            for i in range(tiles):
                at_cols = pl.ds(i * TILE, TILE)
                gate = jnp.dot(block, gate_w[:, at_cols], preferred_element_type=jnp.float32)
                upper = jnp.dot(block, up_w[:, at_cols], preferred_element_type=jnp.float32)
                value = (jax.nn.silu(gate) * upper).astype(jnp.bfloat16)
                for j, chip in enumerate(chips):
                    yy = (y, oy)[chip[2]]
                    hid[y, chip[0], chip[1], yy, :, at_cols] = value[j * 2 * q:(j + 1) * 2 * q]
                    if number == 0:
                        hid_copy(chip, at_cols).start()

    def ship(chips):
        for chip in chips:
            hid_copy(chip, pl.ds(0, units)).start()

    def core_copy(k, dx):
        return pltpu.make_async_remote_copy(
            src_ref=own.at[k, dx, oc], dst_ref=core_in.at[k, dx],
            send_sem=core_send, recv_sem=core_recv.at[k, dx],
            device_id=peers[2], device_id_type=MESH)

    def push(src, dst, send_sem, recv_sem, dev):
        pltpu.make_async_remote_copy(
            src_ref=src, dst_ref=dst, send_sem=send_sem, recv_sem=recv_sem,
            device_id=dev, device_id_type=MESH).start()

    def outputs_of(*groups):
        size = 4 * q
        name = "".join(f"{k}{dx}" for k, dx in groups)
        with jax.named_scope(f"hid{name}"):
            for k, dx in groups:
                wait_blocks(hid.at[oy, k, dx], recv_sem=hid_recv.at[k, dx])
        with jax.named_scope(f"out{name}"):
            picked = lax.broadcasted_iota(jnp.int32, (size, PAD), 1)
            take = jnp.logical_and(picked % n_ep == ep, picked < 3 * n_ep)
            weights, halves = [], ([], [])
            for k, dx in groups:
                codes = rows[order[k], (x, ox)[dx]].reshape(size, width + PAD)[:, width:].astype(jnp.float32)
                weights.append(jnp.sum(jnp.where(take, codes, 0.0), axis=1, keepdims=True))
                for half in range(2):
                    halves[half].append(hid[half, k, dx].reshape(size, units))
            left, right = jnp.concatenate(halves[0], axis=0), jnp.concatenate(halves[1], axis=0)
            for i in range(cols // TILE):
                at_cols = pl.ds(i * TILE, TILE)
                total = jnp.dot(left, down_w[:units, at_cols], preferred_element_type=jnp.float32)
                total += jnp.dot(right, down_w[units:, at_cols], preferred_element_type=jnp.float32)
                total = total.astype(jnp.bfloat16).astype(jnp.float32)
                for j, (k, dx) in enumerate(groups):
                    value = (total[j * size:(j + 1) * size] * weights[j]).astype(jnp.bfloat16).reshape(2, 2, q, TILE)
                    own[k, dx, 0, :, :, at_cols] = value[:, 0]
                    own[k, dx, 1, :, :, at_cols] = value[:, 1]
        for k, dx in groups:
            core_copy(k, dx).start()

    def over_core(k, dx):
        with jax.named_scope(f"core{k}{dx}"):
            core_copy(k, dx).wait_recv()
        both = own[k, dx, c].astype(jnp.float32) + core_in[k, dx].astype(jnp.float32)
        if dx:
            pair[k] = both.astype(jnp.bfloat16)
            if k:
                push(pair.at[k], x_in.at[k], x_send, x_recv.at[k], peers[1])
            else:
                push(pair.at[0, oy], xy_in, x_send, xy_recv, at(oy, z, ox, c))
                push(pair.at[0, y], x0_in, x_send, x_recv.at[0], peers[1])
        else:
            keep[k] = both
            if k == 0:
                cross[...] = both.astype(jnp.bfloat16)
                push(cross.at[oy], y_in, y_send, y_recv, peers[0])

    def over_x(k):
        with jax.named_scope(f"x{k}"):
            wait_blocks(x_in.at[k], recv_sem=x_recv.at[k])
        part[k] = (keep[k] + x_in[k].astype(jnp.float32)).astype(jnp.bfloat16)
        push(part.at[k, oy], zy_in.at[z], z_send, zy_recv.at[z], at(oy, order[k], x, c))
        push(part.at[k, y], z_in.at[z], z_send, z_recv.at[z], at(y, order[k], x, c))

    mine = (0, 0, 0)
    send_y(mine)
    send_core(mine)
    for k in range(1, nz):
        send(at(y, order[k], x, c), mine, line_send.at[0], far_sem(place(mine)))
    send_x(mine)
    for w in weights[:2]:
        w.wait()
    middle = jnp.logical_or(z == 1, z == 2)

    def take_second():
        take((2, 0, 1))
        send_x((2, 0, 1))

    hidden_of(0, PASSES[0])
    take((0, 0, 1))
    send_x((0, 0, 1))
    take((1, 0, 0))
    send_x((1, 0, 0))
    take((0, 1, 0))
    hidden_of(1, PASSES[1])
    ship(PASSES[1])
    take((1, 0, 1))
    send_x((1, 0, 1))
    take((1, 1, 0))
    take((3, 0, 0))
    send_y((3, 0, 0))
    send_x((3, 0, 0))
    take((2, 0, 0))
    send_x((2, 0, 0))
    pl.when(middle)(take_second)
    take((0, 1, 1))
    hidden_of(2, PASSES[2])
    ship(PASSES[2])
    weights[2].wait()
    pl.when(jnp.logical_not(middle))(take_second)
    take((3, 0, 1))
    send_x((3, 0, 1))
    take((1, 1, 1))
    take((3, 1, 0))
    hidden_of(3, PASSES[3])
    ship(PASSES[3])
    outputs_of((1, 0))
    take((2, 1, 0))
    take((3, 1, 1))
    hidden_of(4, PASSES[4])
    ship(PASSES[4])
    hidden_of(6, PASSES[6])
    over_core(1, 0)
    take((2, 1, 1))
    hidden_of(5, PASSES[5])
    ship(PASSES[5])
    ship(PASSES[6])
    outputs_of((1, 1), (3, 0))
    over_core(1, 1)
    outputs_of((3, 1), (2, 0))
    over_core(3, 0)
    over_core(3, 1)
    over_core(2, 0)
    over_x(1)
    outputs_of((2, 1))
    over_core(2, 1)
    over_x(3)
    outputs_of((0, 0), (0, 1))
    over_core(0, 0)
    over_core(0, 1)
    over_x(2)

    total, other = keep[0, y], jnp.zeros((q, cols), jnp.float32)
    for k in (1, 3):
        with jax.named_scope(f"z{k}"):
            wait_blocks(z_in.at[order[k]], recv_sem=z_recv.at[order[k]])
            wait_blocks(zy_in.at[order[k]], recv_sem=zy_recv.at[order[k]])
        total = total + z_in[order[k]].astype(jnp.float32)
        other = other + zy_in[order[k]].astype(jnp.float32)
    with jax.named_scope("near"):
        wait_blocks(y_in, recv_sem=y_recv)
        wait_blocks(x0_in, recv_sem=x_recv.at[0])
        wait_blocks(xy_in, recv_sem=xy_recv)
    total = total + x0_in[...].astype(jnp.float32)
    other = other + y_in[...].astype(jnp.float32) + xy_in[...].astype(jnp.float32)

    wait_blocks(blocks(2), send_sem=near_send.at[0])
    wait_blocks(blocks(2 * nz), send_sem=near_send.at[1])
    wait_blocks(blocks(4 * nz), send_sem=near_send.at[2])
    wait_blocks(blocks(nz - 1), send_sem=line_send.at[0])
    pl.when(z < nz - 1)(lambda: wait_blocks(blocks(1), send_sem=line_send.at[1]))
    pl.when(z > 0)(lambda: wait_blocks(blocks(1), send_sem=line_send.at[2]))
    pl.when(jnp.logical_or(z == 1, z == 2))(lambda: wait_blocks(blocks(1), send_sem=line_send.at[3]))
    wait_blocks(hid.at[y], send_sem=hid_send)
    wait_blocks(own.reshape(nz * 4, 2, q, cols).at[pl.ds(0, 2 * nz)], send_sem=core_send)
    wait_blocks(pair, send_sem=x_send)
    wait_blocks(part.at[pl.ds(1, nz - 1)], send_sem=z_send)
    wait_blocks(y_in, send_sem=y_send)
    with jax.named_scope("last"):
        wait_blocks(z_in.at[order[2]], recv_sem=z_recv.at[order[2]])
        wait_blocks(zy_in.at[order[2]], recv_sem=zy_recv.at[order[2]])
    total = total + z_in[order[2]].astype(jnp.float32)
    other = other + zy_in[order[2]].astype(jnp.float32)
    out_ref[:, pl.ds(pl.multiple_of(y * cols, cols), cols)] = total.astype(jnp.bfloat16)
    out_ref[:, pl.ds(pl.multiple_of(oy * cols, cols), cols)] = other.astype(jnp.bfloat16)


def dense_body(tokens, logits, expert_ids, w_gate_up, w_down):
    nz = NZ
    q, width = tokens.shape
    picks = logits.shape[1]
    units = w_gate_up.shape[3]
    cols = w_down.shape[2]
    bf, sem = jnp.bfloat16, pltpu.SemaphoreType.DMA
    vmem = pl.BlockSpec(memory_space=pltpu.VMEM)
    hbm = pl.BlockSpec(memory_space=pl.ANY)
    return pl.pallas_call(
        dense_kernel,
        out_shape=pltpu.VMEM((q, width), bf),
        in_specs=[hbm] * 5,
        out_specs=vmem,
        scratch_shapes=[
            pltpu.VMEM((nz, 2, 2, 2, q, width + PAD), bf),
            pltpu.VMEM((picks, q), jnp.float32),
            pltpu.VMEM((picks, q), jnp.int32),
            pltpu.VMEM((width, units), bf),
            pltpu.VMEM((width, units), bf),
            pltpu.VMEM((2 * units, cols), bf),
            pltpu.VMEM((2, nz, 2, 2, 2 * q, units), bf),
            pltpu.VMEM((nz, 2, 2, 2, q, cols), bf),
            pltpu.VMEM((nz, 2, 2, q, cols), bf),
            pltpu.VMEM((nz, 2, q, cols), bf),
            pltpu.VMEM((nz, 2, q, cols), jnp.float32),
            pltpu.VMEM((nz, 2, q, cols), bf),
            pltpu.VMEM((nz, 2, q, cols), bf),
            pltpu.VMEM((nz, q, cols), bf),
            pltpu.VMEM((nz, q, cols), bf),
            pltpu.VMEM((2, q, cols), bf),
            pltpu.VMEM((q, cols), bf),
            pltpu.VMEM((q, cols), bf),
            pltpu.VMEM((q, cols), bf),
            sem((6,)),
            sem((3,)), sem((4,)), sem((4 * nz,)), sem((len(PASSES),)),
            sem, sem((nz, 2)),
            sem, sem((nz, 2)),
            sem, sem((nz,)),
            sem, sem((nz,)), sem((nz,)),
            sem, sem, sem,
        ],
        compiler_params=pltpu.CompilerParams(
            collective_id=0, has_side_effects=True, vmem_limit_bytes=58 * 1024 * 1024
        ),
    )(tokens, logits.T, expert_ids.T, w_gate_up, w_down)


def body(tokens, logits, expert_ids, w_gate_up, w_down):
    expert_count = lax.axis_size("ep")
    queue_len, picks = expert_ids.shape
    features = tokens.shape[1]
    capacity = max(2, min(queue_len, 2 * queue_len * picks // expert_count))
    if capacity == queue_len and lax.axis_size("rep") == 2 and expert_count == 4 * NZ:
        return dense_body(tokens, logits, expert_ids, w_gate_up, w_down)
    slot_total = expert_count * capacity
    onehot = slot_plan(expert_ids, expert_count, capacity)
    scaled = jnp.exp(logits)
    weights = scaled / jnp.sum(scaled, axis=1, keepdims=True)
    combine = jnp.sum(weights[:, :, None] * onehot.astype(jnp.float32), axis=1)
    gate_weight = w_gate_up[0, 0]
    up_weight = w_gate_up[0, 1]
    down_weight = w_down[0]
    received = to_owners(dispatch_rows(onehot, tokens).reshape(expert_count, capacity, features))
    slot_rows = received.reshape(slot_total, features)
    portion = lax.all_gather(slot_rows, "rep", axis=0, tiled=True)
    gate_part = jnp.dot(portion, gate_weight, preferred_element_type=jnp.float32)
    upper = jnp.dot(portion, up_weight, preferred_element_type=jnp.float32)
    quarter = (jax.nn.silu(gate_part) * upper).astype(jnp.bfloat16)
    hidden = full_units(quarter)
    partial_out = jnp.dot(hidden, down_weight, preferred_element_type=jnp.float32).astype(
        jnp.bfloat16
    )
    own_rows = lax.all_to_all(partial_out, "rep", split_axis=0, concat_axis=1, tiled=True)
    returned = to_sources(own_rows.reshape(expert_count, capacity, features))
    values = returned.reshape(slot_total, features)
    mixed = jnp.dot(combine, values.astype(jnp.float32), precision=lax.Precision.HIGHEST)
    return mixed.astype(jnp.bfloat16)


def solution(mesh):
    in_specs = (
        P(("rep", "ep"), None),
        P(("rep", "ep"), None),
        P(("rep", "ep"), None),
        P("ep", None, None, "rep"),
        P("ep", None, "rep"),
    )
    out_specs = P(("rep", "ep"), None)
    return jax.shard_map(body, mesh=mesh, in_specs=in_specs, out_specs=out_specs, check_vma=False)
```

```python
import jax
import jax.numpy as jnp
from jax import lax
from jax.experimental import pallas as pl
from jax.experimental.pallas import tpu as pltpu
from jax.sharding import PartitionSpec as P


def slot_plan(choice_ids, expert_count, capacity):
    queue_len, picks = choice_ids.shape
    flat_ids = choice_ids.reshape(queue_len * picks)
    position = jnp.arange(queue_len * picks, dtype=jnp.int32)
    earlier = (flat_ids[:, None] == flat_ids[None, :]) & (position[None, :] < position[:, None])
    slot_rank = jnp.sum(earlier.astype(jnp.int32), axis=1)
    target = flat_ids * capacity + slot_rank
    columns = jnp.arange(expert_count * capacity, dtype=jnp.int32)
    onehot = target[:, None] == columns[None, :]
    return onehot.reshape(queue_len, picks, expert_count * capacity)


def dispatch_rows(onehot, tokens):
    placing = jnp.sum(onehot.astype(jnp.bfloat16), axis=1)
    return jnp.dot(placing.T, tokens, preferred_element_type=jnp.float32).astype(jnp.bfloat16)


def to_owners(outgoing):
    return lax.all_to_all(outgoing, "ep", split_axis=0, concat_axis=0, tiled=True)


def to_sources(results):
    return lax.all_to_all(results, "ep", split_axis=0, concat_axis=0, tiled=True)


def full_units(quarter):
    return lax.all_gather(quarter, "rep", axis=1, tiled=True)


MESH = pl.DeviceIdType.MESH
PAD = 128


TILE = 256


NZ = 4
PASSES = [
    [(0, 0, 0)],
    [(1, 0, 0), (0, 1, 0)],
    [(1, 1, 0), (1, 0, 1), (2, 0, 0), (3, 0, 0)],
    [(1, 1, 1), (3, 1, 0), (3, 0, 1), (2, 0, 1)],
    [(3, 1, 1), (2, 1, 0), (2, 1, 1)],
    [(0, 0, 1), (0, 1, 1)],
]


def dense_kernel(tok_ref, logit_ref, ids_ref, wgu_ref, wd_ref, out_ref,
                 rows, logit_v, ids_v, gate_w, up_w, down_w, hid, own, core_in, pair, keep, x_in,
                 part, z_in, zy_in, cross, y_in, x0_in, xy_in,
                 w_sem, near_send, line_send, far_recv, pass_recv, hid_send, hid_recv, core_send, core_recv,
                 x_send, x_recv, z_send, z_recv, zy_recv, y_send, y_recv, xy_recv):
    y = lax.axis_index("rep")
    ep = lax.axis_index("ep")
    z, x, c = ep // 4, (ep // 2) % 2, ep % 2
    oy, ox, oc = 1 - y, 1 - x, 1 - c
    q, width = tok_ref.shape
    units = gate_w.shape[1]
    cols = down_w.shape[1]
    nz, n_ep = NZ, 4 * NZ
    tiles = units // TILE

    def at(yy, zz, xx, cc):
        return (yy, zz * 4 + xx * 2 + cc)

    small = [
        pltpu.make_async_copy(logit_ref, logit_v, w_sem.at[0]),
        pltpu.make_async_copy(ids_ref, ids_v, w_sem.at[1]),
        pltpu.make_async_copy(tok_ref, rows.at[z, x, y, c, :, pl.ds(0, width)], w_sem.at[2]),
    ]
    weights = [
        pltpu.make_async_copy(wgu_ref.at[0, 0], gate_w, w_sem.at[3]),
        pltpu.make_async_copy(wgu_ref.at[0, 1], up_w, w_sem.at[4]),
        pltpu.make_async_copy(wd_ref.at[0], down_w, w_sem.at[5]),
    ]
    for w in small + weights:
        w.start()

    barrier = pltpu.get_barrier_semaphore()
    peers = [at(oy, z, x, c), at(y, z, ox, c), at(y, z, x, oc)]
    peers += [at(yy, (z + d) % nz, x, c) for yy in (y, oy) for d in range(1, nz)]
    peers += [at(oy, z, ox, c)]
    for p in peers:
        pl.semaphore_signal(barrier, inc=1, device_id=p, device_id_type=MESH)

    for w in small:
        w.wait()
    scaled = jnp.exp(logit_v[...])
    soft = scaled / jnp.sum(scaled, axis=0, keepdims=True)
    line = lax.broadcasted_iota(jnp.int32, (PAD, q), 0)
    expert, piece = line % n_ep, line // n_ep
    ids = ids_v[...]
    comb = jnp.zeros((PAD, q), jnp.float32)
    for k in range(ids.shape[0]):
        comb = comb + jnp.where(ids[k:k + 1, :] == expert, soft[k:k + 1, :], 0.0)
    hi = comb.astype(jnp.bfloat16).astype(jnp.float32)
    rest = comb - hi
    mid = rest.astype(jnp.bfloat16).astype(jnp.float32)
    low = rest - mid
    coded = jnp.where(piece == 0, hi, jnp.where(piece == 1, mid, jnp.where(piece == 2, low, 0.0)))
    rows[z, x, y, c, :, width:] = coded.T.astype(jnp.bfloat16)
    with jax.named_scope("entry"):
        pl.semaphore_wait(barrier, len(peers))

    near = jnp.minimum(z, nz - 1 - z)
    rising = z < nz - 1 - z
    order = [z]
    for k in range(1, nz):
        d = jnp.where(k <= 2 * near, (k + 1) // 2, k - near)
        sign = jnp.where(k <= 2 * near, -1 if k % 2 else 1, jnp.where(rising, 1, -1))
        order.append(z + sign * d)
    up, down = at(y, jnp.minimum(z + 1, nz - 1), x, c), at(y, jnp.maximum(z - 1, 0), x, c)

    chain = [[(z < nz - 1, up, 1), (z > 0, down, 2)], [(z == 2, up, 3)], [(z == 1, down, 3)]]
    pass_of = {chip: number for number, chips in enumerate(PASSES) for chip in chips}

    def place(chip):
        k, dx, dy = chip
        return order[k], (x, ox)[dx], (y, oy)[dy]

    def send(dev, chip, send_sem, recv_sem):
        block = rows.at[(*place(chip), c)]
        pltpu.make_async_remote_copy(
            src_ref=block, dst_ref=block, send_sem=send_sem, recv_sem=recv_sem,
            device_id=dev, device_id_type=MESH).start()

    def far_sem(s):
        return far_recv.at[(s[0] * 2 + s[1]) * 2 + s[2]]

    def wait_blocks(ref, send_sem=None, recv_sem=None):
        copy = pltpu.make_async_remote_copy(
            src_ref=ref, dst_ref=ref, send_sem=send_sem if recv_sem is None else recv_sem,
            recv_sem=send_sem if recv_sem is None else recv_sem,
            device_id=peers[0], device_id_type=MESH)
        if recv_sem is None:
            copy.wait_send()
        else:
            copy.wait_recv()

    def arrive(chip):
        wait_blocks(rows.at[(*place(chip), c)], recv_sem=far_sem(place(chip)))

    def blocks(count):
        return rows.reshape(8 * nz, q, width + PAD).at[pl.ds(0, count)]

    def arrive_pass(number):
        wait_blocks(blocks(len(PASSES[number])), recv_sem=pass_recv.at[number])

    def send_y(chip):
        send(peers[0], chip, near_send.at[0], far_sem(place(chip)))

    def send_x(chip):
        send(peers[1], chip, near_send.at[1], far_sem(place(chip)))

    def send_core(chip):
        send(peers[2], chip, near_send.at[2], pass_recv.at[pass_of[chip]])

    def take(chip):
        k, dx, dy = chip
        with jax.named_scope(f"fw{k}{dx}{dy}"):
            arrive(chip)
        send_core(chip)
        if (dx, dy) == (0, 1) and k < 3:
            for go, dev, sem in chain[k]:
                pl.when(go)(lambda: send(dev, chip, line_send.at[sem], far_sem(place(chip))))

    def hid_copy(chip, at_cols):
        k, dx = chip[:2]
        part_of = hid.at[y, k, dx, (y, oy)[chip[2]], :, at_cols]
        return pltpu.make_async_remote_copy(
            src_ref=part_of, dst_ref=part_of,
            send_sem=hid_send, recv_sem=hid_recv.at[k, dx],
            device_id=peers[0], device_id_type=MESH)

    def hidden_of(number, chips):
        with jax.named_scope(f"rows{number}"):
            arrive_pass(number)
        with jax.named_scope(f"hidden{number}"):
            block = jnp.concatenate([rows[(*place(chip),)].reshape(2 * q, width + PAD)[:, :width] for chip in chips], axis=0)
            for i in range(tiles):
                at_cols = pl.ds(i * TILE, TILE)
                gate = jnp.dot(block, gate_w[:, at_cols], preferred_element_type=jnp.float32)
                upper = jnp.dot(block, up_w[:, at_cols], preferred_element_type=jnp.float32)
                value = (jax.nn.silu(gate) * upper).astype(jnp.bfloat16)
                for j, chip in enumerate(chips):
                    yy = (y, oy)[chip[2]]
                    hid[y, chip[0], chip[1], yy, :, at_cols] = value[j * 2 * q:(j + 1) * 2 * q]
                    if number == 0:
                        hid_copy(chip, at_cols).start()

    def ship(chips):
        for chip in chips:
            hid_copy(chip, pl.ds(0, units)).start()

    def core_copy(k, dx):
        return pltpu.make_async_remote_copy(
            src_ref=own.at[k, dx, oc], dst_ref=core_in.at[k, dx],
            send_sem=core_send, recv_sem=core_recv.at[k, dx],
            device_id=peers[2], device_id_type=MESH)

    def push(src, dst, send_sem, recv_sem, dev):
        pltpu.make_async_remote_copy(
            src_ref=src, dst_ref=dst, send_sem=send_sem, recv_sem=recv_sem,
            device_id=dev, device_id_type=MESH).start()

    def outputs_of(*groups):
        size = 4 * q
        name = "".join(f"{k}{dx}" for k, dx in groups)
        with jax.named_scope(f"hid{name}"):
            for k, dx in groups:
                wait_blocks(hid.at[oy, k, dx], recv_sem=hid_recv.at[k, dx])
        with jax.named_scope(f"out{name}"):
            picked = lax.broadcasted_iota(jnp.int32, (size, PAD), 1)
            take = jnp.logical_and(picked % n_ep == ep, picked < 3 * n_ep)
            weights, halves = [], ([], [])
            for k, dx in groups:
                codes = rows[order[k], (x, ox)[dx]].reshape(size, width + PAD)[:, width:].astype(jnp.float32)
                weights.append(jnp.sum(jnp.where(take, codes, 0.0), axis=1, keepdims=True))
                for half in range(2):
                    halves[half].append(hid[half, k, dx].reshape(size, units))
            left, right = jnp.concatenate(halves[0], axis=0), jnp.concatenate(halves[1], axis=0)
            for i in range(cols // TILE):
                at_cols = pl.ds(i * TILE, TILE)
                total = jnp.dot(left, down_w[:units, at_cols], preferred_element_type=jnp.float32)
                total += jnp.dot(right, down_w[units:, at_cols], preferred_element_type=jnp.float32)
                total = total.astype(jnp.bfloat16).astype(jnp.float32)
                for j, (k, dx) in enumerate(groups):
                    value = (total[j * size:(j + 1) * size] * weights[j]).astype(jnp.bfloat16).reshape(2, 2, q, TILE)
                    own[k, dx, 0, :, :, at_cols] = value[:, 0]
                    own[k, dx, 1, :, :, at_cols] = value[:, 1]
        for k, dx in groups:
            core_copy(k, dx).start()

    def over_core(k, dx):
        with jax.named_scope(f"core{k}{dx}"):
            core_copy(k, dx).wait_recv()
        both = own[k, dx, c].astype(jnp.float32) + core_in[k, dx].astype(jnp.float32)
        if dx:
            pair[k] = both.astype(jnp.bfloat16)
            if k:
                push(pair.at[k], x_in.at[k], x_send, x_recv.at[k], peers[1])
            else:
                push(pair.at[0, oy], xy_in, x_send, xy_recv, at(oy, z, ox, c))
                push(pair.at[0, y], x0_in, x_send, x_recv.at[0], peers[1])
        else:
            keep[k] = both
            if k == 0:
                cross[...] = both.astype(jnp.bfloat16)
                push(cross.at[oy], y_in, y_send, y_recv, peers[0])

    def over_x(k):
        with jax.named_scope(f"x{k}"):
            wait_blocks(x_in.at[k], recv_sem=x_recv.at[k])
        part[k] = (keep[k] + x_in[k].astype(jnp.float32)).astype(jnp.bfloat16)
        push(part.at[k, oy], zy_in.at[z], z_send, zy_recv.at[z], at(oy, order[k], x, c))
        push(part.at[k, y], z_in.at[z], z_send, z_recv.at[z], at(y, order[k], x, c))

    mine = (0, 0, 0)
    send_y(mine)
    send_core(mine)
    for k in range(1, nz):
        send(at(y, order[k], x, c), mine, line_send.at[0], far_sem(place(mine)))
    send_x(mine)
    for w in weights[:2]:
        w.wait()
    middle = jnp.logical_or(z == 1, z == 2)

    def take_second():
        take((2, 0, 1))
        send_x((2, 0, 1))

    hidden_of(0, PASSES[0])
    take((0, 0, 1))
    send_x((0, 0, 1))
    take((1, 0, 0))
    send_x((1, 0, 0))
    take((0, 1, 0))
    hidden_of(1, PASSES[1])
    ship(PASSES[1])
    take((1, 0, 1))
    send_x((1, 0, 1))
    take((1, 1, 0))
    take((3, 0, 0))
    send_y((3, 0, 0))
    send_x((3, 0, 0))
    take((2, 0, 0))
    send_x((2, 0, 0))
    pl.when(middle)(take_second)
    take((0, 1, 1))
    hidden_of(2, PASSES[2])
    ship(PASSES[2])
    weights[2].wait()
    pl.when(jnp.logical_not(middle))(take_second)
    take((3, 0, 1))
    send_x((3, 0, 1))
    take((1, 1, 1))
    take((3, 1, 0))
    hidden_of(3, PASSES[3])
    ship(PASSES[3])
    hidden_of(5, PASSES[5])
    outputs_of((1, 0))
    take((2, 1, 0))
    take((3, 1, 1))
    take((2, 1, 1))
    hidden_of(4, PASSES[4])
    ship(PASSES[4])
    over_core(1, 0)
    outputs_of((1, 1), (3, 0))
    ship(PASSES[5])
    over_core(1, 1)
    over_core(3, 0)
    outputs_of((3, 1))
    over_core(3, 1)
    outputs_of((2, 0), (2, 1))
    pl.when(z != 2)(lambda: over_x(1))
    over_core(2, 0)
    over_core(2, 1)
    over_x(3)
    outputs_of((0, 0), (0, 1))
    pl.when(z == 2)(lambda: over_x(1))
    over_core(0, 0)
    over_core(0, 1)
    over_x(2)

    total, other = keep[0, y], jnp.zeros((q, cols), jnp.float32)
    for k in (1, 3):
        with jax.named_scope(f"z{k}"):
            wait_blocks(z_in.at[order[k]], recv_sem=z_recv.at[order[k]])
            wait_blocks(zy_in.at[order[k]], recv_sem=zy_recv.at[order[k]])
        total = total + z_in[order[k]].astype(jnp.float32)
        other = other + zy_in[order[k]].astype(jnp.float32)
    with jax.named_scope("near"):
        wait_blocks(y_in, recv_sem=y_recv)
        wait_blocks(x0_in, recv_sem=x_recv.at[0])
        wait_blocks(xy_in, recv_sem=xy_recv)
    total = total + x0_in[...].astype(jnp.float32)
    other = other + y_in[...].astype(jnp.float32) + xy_in[...].astype(jnp.float32)

    wait_blocks(blocks(2), send_sem=near_send.at[0])
    wait_blocks(blocks(2 * nz), send_sem=near_send.at[1])
    wait_blocks(blocks(4 * nz), send_sem=near_send.at[2])
    wait_blocks(blocks(nz - 1), send_sem=line_send.at[0])
    pl.when(z < nz - 1)(lambda: wait_blocks(blocks(1), send_sem=line_send.at[1]))
    pl.when(z > 0)(lambda: wait_blocks(blocks(1), send_sem=line_send.at[2]))
    pl.when(jnp.logical_or(z == 1, z == 2))(lambda: wait_blocks(blocks(1), send_sem=line_send.at[3]))
    wait_blocks(hid.at[y], send_sem=hid_send)
    wait_blocks(own.reshape(nz * 4, 2, q, cols).at[pl.ds(0, 2 * nz)], send_sem=core_send)
    wait_blocks(pair, send_sem=x_send)
    wait_blocks(part.at[pl.ds(1, nz - 1)], send_sem=z_send)
    wait_blocks(y_in, send_sem=y_send)
    with jax.named_scope("last"):
        wait_blocks(z_in.at[order[2]], recv_sem=z_recv.at[order[2]])
        wait_blocks(zy_in.at[order[2]], recv_sem=zy_recv.at[order[2]])
    total = total + z_in[order[2]].astype(jnp.float32)
    other = other + zy_in[order[2]].astype(jnp.float32)
    out_ref[:, pl.ds(pl.multiple_of(y * cols, cols), cols)] = total.astype(jnp.bfloat16)
    out_ref[:, pl.ds(pl.multiple_of(oy * cols, cols), cols)] = other.astype(jnp.bfloat16)


def dense_body(tokens, logits, expert_ids, w_gate_up, w_down):
    nz = NZ
    q, width = tokens.shape
    picks = logits.shape[1]
    units = w_gate_up.shape[3]
    cols = w_down.shape[2]
    bf, sem = jnp.bfloat16, pltpu.SemaphoreType.DMA
    vmem = pl.BlockSpec(memory_space=pltpu.VMEM)
    hbm = pl.BlockSpec(memory_space=pl.ANY)
    return pl.pallas_call(
        dense_kernel,
        out_shape=pltpu.VMEM((q, width), bf),
        in_specs=[hbm] * 5,
        out_specs=vmem,
        scratch_shapes=[
            pltpu.VMEM((nz, 2, 2, 2, q, width + PAD), bf),
            pltpu.VMEM((picks, q), jnp.float32),
            pltpu.VMEM((picks, q), jnp.int32),
            pltpu.VMEM((width, units), bf),
            pltpu.VMEM((width, units), bf),
            pltpu.VMEM((2 * units, cols), bf),
            pltpu.VMEM((2, nz, 2, 2, 2 * q, units), bf),
            pltpu.VMEM((nz, 2, 2, 2, q, cols), bf),
            pltpu.VMEM((nz, 2, 2, q, cols), bf),
            pltpu.VMEM((nz, 2, q, cols), bf),
            pltpu.VMEM((nz, 2, q, cols), jnp.float32),
            pltpu.VMEM((nz, 2, q, cols), bf),
            pltpu.VMEM((nz, 2, q, cols), bf),
            pltpu.VMEM((nz, q, cols), bf),
            pltpu.VMEM((nz, q, cols), bf),
            pltpu.VMEM((2, q, cols), bf),
            pltpu.VMEM((q, cols), bf),
            pltpu.VMEM((q, cols), bf),
            pltpu.VMEM((q, cols), bf),
            sem((6,)),
            sem((3,)), sem((4,)), sem((4 * nz,)), sem((len(PASSES),)),
            sem, sem((nz, 2)),
            sem, sem((nz, 2)),
            sem, sem((nz,)),
            sem, sem((nz,)), sem((nz,)),
            sem, sem, sem,
        ],
        compiler_params=pltpu.CompilerParams(
            collective_id=0, has_side_effects=True, vmem_limit_bytes=58 * 1024 * 1024
        ),
    )(tokens, logits.T, expert_ids.T, w_gate_up, w_down)


def body(tokens, logits, expert_ids, w_gate_up, w_down):
    expert_count = lax.axis_size("ep")
    queue_len, picks = expert_ids.shape
    features = tokens.shape[1]
    capacity = max(2, min(queue_len, 2 * queue_len * picks // expert_count))
    if capacity == queue_len and lax.axis_size("rep") == 2 and expert_count == 4 * NZ:
        return dense_body(tokens, logits, expert_ids, w_gate_up, w_down)
    slot_total = expert_count * capacity
    onehot = slot_plan(expert_ids, expert_count, capacity)
    scaled = jnp.exp(logits)
    weights = scaled / jnp.sum(scaled, axis=1, keepdims=True)
    combine = jnp.sum(weights[:, :, None] * onehot.astype(jnp.float32), axis=1)
    gate_weight = w_gate_up[0, 0]
    up_weight = w_gate_up[0, 1]
    down_weight = w_down[0]
    received = to_owners(dispatch_rows(onehot, tokens).reshape(expert_count, capacity, features))
    slot_rows = received.reshape(slot_total, features)
    portion = lax.all_gather(slot_rows, "rep", axis=0, tiled=True)
    gate_part = jnp.dot(portion, gate_weight, preferred_element_type=jnp.float32)
    upper = jnp.dot(portion, up_weight, preferred_element_type=jnp.float32)
    quarter = (jax.nn.silu(gate_part) * upper).astype(jnp.bfloat16)
    hidden = full_units(quarter)
    partial_out = jnp.dot(hidden, down_weight, preferred_element_type=jnp.float32).astype(
        jnp.bfloat16
    )
    own_rows = lax.all_to_all(partial_out, "rep", split_axis=0, concat_axis=1, tiled=True)
    returned = to_sources(own_rows.reshape(expert_count, capacity, features))
    values = returned.reshape(slot_total, features)
    mixed = jnp.dot(combine, values.astype(jnp.float32), precision=lax.Precision.HIGHEST)
    return mixed.astype(jnp.bfloat16)


def solution(mesh):
    in_specs = (
        P(("rep", "ep"), None),
        P(("rep", "ep"), None),
        P(("rep", "ep"), None),
        P("ep", None, None, "rep"),
        P("ep", None, "rep"),
    )
    out_specs = P(("rep", "ep"), None)
    return jax.shard_map(body, mesh=mesh, in_specs=in_specs, out_specs=out_specs, check_vma=False)
```

```python
import jax
import jax.numpy as jnp
from jax import lax
from jax.experimental import pallas as pl
from jax.experimental.pallas import tpu as pltpu
from jax.sharding import PartitionSpec as P


def slot_plan(choice_ids, expert_count, capacity):
    queue_len, picks = choice_ids.shape
    flat_ids = choice_ids.reshape(queue_len * picks)
    position = jnp.arange(queue_len * picks, dtype=jnp.int32)
    earlier = (flat_ids[:, None] == flat_ids[None, :]) & (position[None, :] < position[:, None])
    slot_rank = jnp.sum(earlier.astype(jnp.int32), axis=1)
    target = flat_ids * capacity + slot_rank
    columns = jnp.arange(expert_count * capacity, dtype=jnp.int32)
    onehot = target[:, None] == columns[None, :]
    return onehot.reshape(queue_len, picks, expert_count * capacity)


def dispatch_rows(onehot, tokens):
    placing = jnp.sum(onehot.astype(jnp.bfloat16), axis=1)
    return jnp.dot(placing.T, tokens, preferred_element_type=jnp.float32).astype(jnp.bfloat16)


def to_owners(outgoing):
    return lax.all_to_all(outgoing, "ep", split_axis=0, concat_axis=0, tiled=True)


def to_sources(results):
    return lax.all_to_all(results, "ep", split_axis=0, concat_axis=0, tiled=True)


def full_units(quarter):
    return lax.all_gather(quarter, "rep", axis=1, tiled=True)


MESH = pl.DeviceIdType.MESH
PAD = 128


TILE = 256


NZ = 4
PASSES = [
    [(0, 0, 0)],
    [(0, 0, 1), (1, 0, 0), (0, 1, 0)],
    [(1, 1, 0), (1, 0, 1), (2, 0, 0), (3, 0, 0)],
    [(1, 1, 1), (3, 1, 0), (3, 0, 1), (2, 0, 1)],
    [(3, 1, 1), (2, 1, 0), (2, 1, 1)],
    [(0, 1, 1)],
]


def dense_kernel(tok_ref, logit_ref, ids_ref, wgu_ref, wd_ref, out_ref,
                 rows, logit_v, ids_v, gate_w, up_w, down_w, hid, own, core_in, pair, keep, x_in,
                 part, z_in, zy_in, cross, y_in, x0_in, xy_in,
                 w_sem, near_send, line_send, far_recv, pass_recv, hid_send, hid_recv, core_send, core_recv,
                 x_send, x_recv, z_send, z_recv, zy_recv, y_send, y_recv, xy_recv):
    y = lax.axis_index("rep")
    ep = lax.axis_index("ep")
    z, x, c = ep // 4, (ep // 2) % 2, ep % 2
    oy, ox, oc = 1 - y, 1 - x, 1 - c
    q, width = tok_ref.shape
    units = gate_w.shape[1]
    cols = down_w.shape[1]
    nz, n_ep = NZ, 4 * NZ
    tiles = units // TILE

    def at(yy, zz, xx, cc):
        return (yy, zz * 4 + xx * 2 + cc)

    small = [
        pltpu.make_async_copy(logit_ref, logit_v, w_sem.at[0]),
        pltpu.make_async_copy(ids_ref, ids_v, w_sem.at[1]),
        pltpu.make_async_copy(tok_ref, rows.at[z, x, y, c, :, pl.ds(0, width)], w_sem.at[2]),
    ]
    weights = [
        pltpu.make_async_copy(wgu_ref.at[0, 0], gate_w, w_sem.at[3]),
        pltpu.make_async_copy(wgu_ref.at[0, 1], up_w, w_sem.at[4]),
        pltpu.make_async_copy(wd_ref.at[0], down_w, w_sem.at[5]),
    ]
    for w in small + weights:
        w.start()

    barrier = pltpu.get_barrier_semaphore()
    peers = [at(oy, z, x, c), at(y, z, ox, c), at(y, z, x, oc)]
    peers += [at(yy, (z + d) % nz, x, c) for yy in (y, oy) for d in range(1, nz)]
    peers += [at(oy, z, ox, c)]
    for p in peers:
        pl.semaphore_signal(barrier, inc=1, device_id=p, device_id_type=MESH)

    for w in small:
        w.wait()
    scaled = jnp.exp(logit_v[...])
    soft = scaled / jnp.sum(scaled, axis=0, keepdims=True)
    line = lax.broadcasted_iota(jnp.int32, (PAD, q), 0)
    expert, piece = line % n_ep, line // n_ep
    ids = ids_v[...]
    comb = jnp.zeros((PAD, q), jnp.float32)
    for k in range(ids.shape[0]):
        comb = comb + jnp.where(ids[k:k + 1, :] == expert, soft[k:k + 1, :], 0.0)
    hi = comb.astype(jnp.bfloat16).astype(jnp.float32)
    rest = comb - hi
    mid = rest.astype(jnp.bfloat16).astype(jnp.float32)
    low = rest - mid
    coded = jnp.where(piece == 0, hi, jnp.where(piece == 1, mid, jnp.where(piece == 2, low, 0.0)))
    rows[z, x, y, c, :, width:] = coded.T.astype(jnp.bfloat16)
    with jax.named_scope("entry"):
        pl.semaphore_wait(barrier, len(peers))

    near = jnp.minimum(z, nz - 1 - z)
    rising = z < nz - 1 - z
    order = [z]
    for k in range(1, nz):
        d = jnp.where(k <= 2 * near, (k + 1) // 2, k - near)
        sign = jnp.where(k <= 2 * near, -1 if k % 2 else 1, jnp.where(rising, 1, -1))
        order.append(z + sign * d)
    up, down = at(y, jnp.minimum(z + 1, nz - 1), x, c), at(y, jnp.maximum(z - 1, 0), x, c)

    chain = [[(z < nz - 1, up, 1), (z > 0, down, 2)], [(z == 2, up, 3)], [(z == 1, down, 3)]]
    pass_of = {chip: number for number, chips in enumerate(PASSES) for chip in chips}

    mine = (0, 0, 0)

    def place(chip):
        k, dx, dy = chip
        return order[k], (x, ox)[dx], (y, oy)[dy]

    def send(dev, chip, send_sem, recv_sem):
        block = rows.at[(*place(chip), c)]
        pltpu.make_async_remote_copy(
            src_ref=block, dst_ref=block, send_sem=send_sem, recv_sem=recv_sem,
            device_id=dev, device_id_type=MESH).start()

    def far_sem(s):
        return far_recv.at[(s[0] * 2 + s[1]) * 2 + s[2]]

    def wait_blocks(ref, send_sem=None, recv_sem=None):
        copy = pltpu.make_async_remote_copy(
            src_ref=ref, dst_ref=ref, send_sem=send_sem if recv_sem is None else recv_sem,
            recv_sem=send_sem if recv_sem is None else recv_sem,
            device_id=peers[0], device_id_type=MESH)
        if recv_sem is None:
            copy.wait_send()
        else:
            copy.wait_recv()

    def arrive(chip):
        wait_blocks(rows.at[(*place(chip), c)], recv_sem=far_sem(place(chip)))

    def blocks(count):
        return rows.reshape(8 * nz, q, width + PAD).at[pl.ds(0, count)]

    def arrive_pass(number):
        wait_blocks(blocks(len(PASSES[number])), recv_sem=pass_recv.at[number])

    def send_y(chip):
        send(peers[0], chip, near_send.at[0], far_sem(place(chip)))

    def send_x(chip):
        send(peers[1], chip, near_send.at[1], far_sem(place(chip)))

    def send_core(chip):
        send(peers[2], chip, near_send.at[2], pass_recv.at[pass_of[chip]])

    def take(chip):
        k, dx, dy = chip
        with jax.named_scope(f"fw{k}{dx}{dy}"):
            arrive(chip)
        send_core(chip)
        if (dx, dy) == (0, 1) and k < 3:
            for go, dev, sem in chain[k]:
                pl.when(go)(lambda: send(dev, chip, line_send.at[sem], far_sem(place(chip))))

    def hid_copy(chip, at_cols):
        k, dx = chip[:2]
        part_of = hid.at[y, k, dx, (y, oy)[chip[2]], :, at_cols]
        return pltpu.make_async_remote_copy(
            src_ref=part_of, dst_ref=part_of,
            send_sem=hid_send, recv_sem=hid_recv.at[k, dx],
            device_id=peers[0], device_id_type=MESH)

    def hidden_of(number, chips):
        with jax.named_scope(f"rows{number}"):
            arrive_pass(number)
        with jax.named_scope(f"hidden{number}"):
            block = jnp.concatenate([rows[(*place(chip),)].reshape(2 * q, width + PAD)[:, :width] for chip in chips], axis=0)
            for i in range(tiles):
                at_cols = pl.ds(i * TILE, TILE)
                gate = jnp.dot(block, gate_w[:, at_cols], preferred_element_type=jnp.float32)
                upper = jnp.dot(block, up_w[:, at_cols], preferred_element_type=jnp.float32)
                value = (jax.nn.silu(gate) * upper).astype(jnp.bfloat16)
                for j, chip in enumerate(chips):
                    yy = (y, oy)[chip[2]]
                    hid[y, chip[0], chip[1], yy, :, at_cols] = value[j * 2 * q:(j + 1) * 2 * q]
                    if number == 0:
                        hid_copy(chip, at_cols).start()
                        if i == 0:
                            send(at(oy, z, ox, c), mine, near_send.at[1], far_sem(place(mine)))

    def ship(chips):
        for chip in chips:
            hid_copy(chip, pl.ds(0, units)).start()

    def core_copy(k, dx):
        return pltpu.make_async_remote_copy(
            src_ref=own.at[k, dx, oc], dst_ref=core_in.at[k, dx],
            send_sem=core_send, recv_sem=core_recv.at[k, dx],
            device_id=peers[2], device_id_type=MESH)

    def push(src, dst, send_sem, recv_sem, dev):
        pltpu.make_async_remote_copy(
            src_ref=src, dst_ref=dst, send_sem=send_sem, recv_sem=recv_sem,
            device_id=dev, device_id_type=MESH).start()

    def outputs_of(*groups):
        size = 4 * q
        name = "".join(f"{k}{dx}" for k, dx in groups)
        with jax.named_scope(f"hid{name}"):
            for k, dx in groups:
                wait_blocks(hid.at[oy, k, dx], recv_sem=hid_recv.at[k, dx])
        with jax.named_scope(f"out{name}"):
            picked = lax.broadcasted_iota(jnp.int32, (size, PAD), 1)
            take = jnp.logical_and(picked % n_ep == ep, picked < 3 * n_ep)
            weights, halves = [], ([], [])
            for k, dx in groups:
                codes = rows[order[k], (x, ox)[dx]].reshape(size, width + PAD)[:, width:].astype(jnp.float32)
                weights.append(jnp.sum(jnp.where(take, codes, 0.0), axis=1, keepdims=True))
                for half in range(2):
                    halves[half].append(hid[half, k, dx].reshape(size, units))
            left, right = jnp.concatenate(halves[0], axis=0), jnp.concatenate(halves[1], axis=0)
            for i in range(cols // TILE):
                at_cols = pl.ds(i * TILE, TILE)
                total = jnp.dot(left, down_w[:units, at_cols], preferred_element_type=jnp.float32)
                total += jnp.dot(right, down_w[units:, at_cols], preferred_element_type=jnp.float32)
                total = total.astype(jnp.bfloat16).astype(jnp.float32)
                for j, (k, dx) in enumerate(groups):
                    value = (total[j * size:(j + 1) * size] * weights[j]).astype(jnp.bfloat16).reshape(2, 2, q, TILE)
                    own[k, dx, 0, :, :, at_cols] = value[:, 0]
                    own[k, dx, 1, :, :, at_cols] = value[:, 1]
        for k, dx in groups:
            core_copy(k, dx).start()

    def over_core(k, dx):
        with jax.named_scope(f"core{k}{dx}"):
            core_copy(k, dx).wait_recv()
        both = own[k, dx, c].astype(jnp.float32) + core_in[k, dx].astype(jnp.float32)
        if dx:
            pair[k] = both.astype(jnp.bfloat16)
            if k:
                push(pair.at[k], x_in.at[k], x_send, x_recv.at[k], peers[1])
            else:
                push(pair.at[0, oy], xy_in, x_send, xy_recv, at(oy, z, ox, c))
                push(pair.at[0, y], x0_in, x_send, x_recv.at[0], peers[1])
        else:
            keep[k] = both
            if k == 0:
                cross[...] = both.astype(jnp.bfloat16)
                push(cross.at[oy], y_in, y_send, y_recv, peers[0])

    def over_x(k):
        with jax.named_scope(f"x{k}"):
            wait_blocks(x_in.at[k], recv_sem=x_recv.at[k])
        part[k] = (keep[k] + x_in[k].astype(jnp.float32)).astype(jnp.bfloat16)
        push(part.at[k, oy], zy_in.at[z], z_send, zy_recv.at[z], at(oy, order[k], x, c))
        push(part.at[k, y], z_in.at[z], z_send, z_recv.at[z], at(y, order[k], x, c))

    send_y(mine)
    send_core(mine)
    for k in range(1, nz):
        send(at(y, order[k], x, c), mine, line_send.at[0], far_sem(place(mine)))
    send_x(mine)
    for w in weights[:2]:
        w.wait()
    middle = jnp.logical_or(z == 1, z == 2)

    def take_second():
        take((2, 0, 1))
        send_x((2, 0, 1))

    hidden_of(0, PASSES[0])
    take((0, 0, 1))
    take((1, 0, 0))
    send_x((1, 0, 0))
    take((0, 1, 0))
    hidden_of(1, PASSES[1])
    ship(PASSES[1])
    take((1, 0, 1))
    send_x((1, 0, 1))
    take((1, 1, 0))
    take((3, 0, 0))
    send_y((3, 0, 0))
    send_x((3, 0, 0))
    take((2, 0, 0))
    send_x((2, 0, 0))
    pl.when(middle)(take_second)
    take((0, 1, 1))
    hidden_of(2, PASSES[2])
    ship(PASSES[2])
    weights[2].wait()
    pl.when(jnp.logical_not(middle))(take_second)
    take((3, 0, 1))
    send_x((3, 0, 1))
    take((1, 1, 1))
    take((3, 1, 0))
    hidden_of(3, PASSES[3])
    ship(PASSES[3])
    hidden_of(5, PASSES[5])
    outputs_of((1, 0), (0, 0))
    take((2, 1, 0))
    take((3, 1, 1))
    take((2, 1, 1))
    hidden_of(4, PASSES[4])
    ship(PASSES[4])
    over_core(1, 0)
    over_core(0, 0)
    outputs_of((1, 1), (3, 0))
    ship(PASSES[5])
    over_core(1, 1)
    over_core(3, 0)
    outputs_of((3, 1))
    over_core(3, 1)
    outputs_of((2, 0), (2, 1))
    pl.when(z != 2)(lambda: over_x(1))
    over_core(2, 0)
    over_core(2, 1)
    over_x(3)
    outputs_of((0, 1))
    pl.when(z == 2)(lambda: over_x(1))
    over_core(0, 1)
    over_x(2)

    total, other = keep[0, y], jnp.zeros((q, cols), jnp.float32)
    for k in (1, 3):
        with jax.named_scope(f"z{k}"):
            wait_blocks(z_in.at[order[k]], recv_sem=z_recv.at[order[k]])
            wait_blocks(zy_in.at[order[k]], recv_sem=zy_recv.at[order[k]])
        total = total + z_in[order[k]].astype(jnp.float32)
        other = other + zy_in[order[k]].astype(jnp.float32)
    with jax.named_scope("near"):
        wait_blocks(y_in, recv_sem=y_recv)
        wait_blocks(x0_in, recv_sem=x_recv.at[0])
        wait_blocks(xy_in, recv_sem=xy_recv)
    total = total + x0_in[...].astype(jnp.float32)
    other = other + y_in[...].astype(jnp.float32) + xy_in[...].astype(jnp.float32)

    wait_blocks(blocks(2), send_sem=near_send.at[0])
    wait_blocks(blocks(2 * nz), send_sem=near_send.at[1])
    wait_blocks(blocks(4 * nz), send_sem=near_send.at[2])
    wait_blocks(blocks(nz - 1), send_sem=line_send.at[0])
    pl.when(z < nz - 1)(lambda: wait_blocks(blocks(1), send_sem=line_send.at[1]))
    pl.when(z > 0)(lambda: wait_blocks(blocks(1), send_sem=line_send.at[2]))
    pl.when(jnp.logical_or(z == 1, z == 2))(lambda: wait_blocks(blocks(1), send_sem=line_send.at[3]))
    wait_blocks(hid.at[y], send_sem=hid_send)
    wait_blocks(own.reshape(nz * 4, 2, q, cols).at[pl.ds(0, 2 * nz)], send_sem=core_send)
    wait_blocks(pair, send_sem=x_send)
    wait_blocks(part.at[pl.ds(1, nz - 1)], send_sem=z_send)
    wait_blocks(y_in, send_sem=y_send)
    with jax.named_scope("last"):
        wait_blocks(z_in.at[order[2]], recv_sem=z_recv.at[order[2]])
        wait_blocks(zy_in.at[order[2]], recv_sem=zy_recv.at[order[2]])
    total = total + z_in[order[2]].astype(jnp.float32)
    other = other + zy_in[order[2]].astype(jnp.float32)
    out_ref[:, pl.ds(pl.multiple_of(y * cols, cols), cols)] = total.astype(jnp.bfloat16)
    out_ref[:, pl.ds(pl.multiple_of(oy * cols, cols), cols)] = other.astype(jnp.bfloat16)


def dense_body(tokens, logits, expert_ids, w_gate_up, w_down):
    nz = NZ
    q, width = tokens.shape
    picks = logits.shape[1]
    units = w_gate_up.shape[3]
    cols = w_down.shape[2]
    bf, sem = jnp.bfloat16, pltpu.SemaphoreType.DMA
    vmem = pl.BlockSpec(memory_space=pltpu.VMEM)
    hbm = pl.BlockSpec(memory_space=pl.ANY)
    return pl.pallas_call(
        dense_kernel,
        out_shape=pltpu.VMEM((q, width), bf),
        in_specs=[hbm] * 5,
        out_specs=vmem,
        scratch_shapes=[
            pltpu.VMEM((nz, 2, 2, 2, q, width + PAD), bf),
            pltpu.VMEM((picks, q), jnp.float32),
            pltpu.VMEM((picks, q), jnp.int32),
            pltpu.VMEM((width, units), bf),
            pltpu.VMEM((width, units), bf),
            pltpu.VMEM((2 * units, cols), bf),
            pltpu.VMEM((2, nz, 2, 2, 2 * q, units), bf),
            pltpu.VMEM((nz, 2, 2, 2, q, cols), bf),
            pltpu.VMEM((nz, 2, 2, q, cols), bf),
            pltpu.VMEM((nz, 2, q, cols), bf),
            pltpu.VMEM((nz, 2, q, cols), jnp.float32),
            pltpu.VMEM((nz, 2, q, cols), bf),
            pltpu.VMEM((nz, 2, q, cols), bf),
            pltpu.VMEM((nz, q, cols), bf),
            pltpu.VMEM((nz, q, cols), bf),
            pltpu.VMEM((2, q, cols), bf),
            pltpu.VMEM((q, cols), bf),
            pltpu.VMEM((q, cols), bf),
            pltpu.VMEM((q, cols), bf),
            sem((6,)),
            sem((3,)), sem((4,)), sem((4 * nz,)), sem((len(PASSES),)),
            sem, sem((nz, 2)),
            sem, sem((nz, 2)),
            sem, sem((nz,)),
            sem, sem((nz,)), sem((nz,)),
            sem, sem, sem,
        ],
        compiler_params=pltpu.CompilerParams(
            collective_id=0, has_side_effects=True, vmem_limit_bytes=58 * 1024 * 1024
        ),
    )(tokens, logits.T, expert_ids.T, w_gate_up, w_down)


def body(tokens, logits, expert_ids, w_gate_up, w_down):
    expert_count = lax.axis_size("ep")
    queue_len, picks = expert_ids.shape
    features = tokens.shape[1]
    capacity = max(2, min(queue_len, 2 * queue_len * picks // expert_count))
    if capacity == queue_len and lax.axis_size("rep") == 2 and expert_count == 4 * NZ:
        return dense_body(tokens, logits, expert_ids, w_gate_up, w_down)
    slot_total = expert_count * capacity
    onehot = slot_plan(expert_ids, expert_count, capacity)
    scaled = jnp.exp(logits)
    weights = scaled / jnp.sum(scaled, axis=1, keepdims=True)
    combine = jnp.sum(weights[:, :, None] * onehot.astype(jnp.float32), axis=1)
    gate_weight = w_gate_up[0, 0]
    up_weight = w_gate_up[0, 1]
    down_weight = w_down[0]
    received = to_owners(dispatch_rows(onehot, tokens).reshape(expert_count, capacity, features))
    slot_rows = received.reshape(slot_total, features)
    portion = lax.all_gather(slot_rows, "rep", axis=0, tiled=True)
    gate_part = jnp.dot(portion, gate_weight, preferred_element_type=jnp.float32)
    upper = jnp.dot(portion, up_weight, preferred_element_type=jnp.float32)
    quarter = (jax.nn.silu(gate_part) * upper).astype(jnp.bfloat16)
    hidden = full_units(quarter)
    partial_out = jnp.dot(hidden, down_weight, preferred_element_type=jnp.float32).astype(
        jnp.bfloat16
    )
    own_rows = lax.all_to_all(partial_out, "rep", split_axis=0, concat_axis=1, tiled=True)
    returned = to_sources(own_rows.reshape(expert_count, capacity, features))
    values = returned.reshape(slot_total, features)
    mixed = jnp.dot(combine, values.astype(jnp.float32), precision=lax.Precision.HIGHEST)
    return mixed.astype(jnp.bfloat16)


def solution(mesh):
    in_specs = (
        P(("rep", "ep"), None),
        P(("rep", "ep"), None),
        P(("rep", "ep"), None),
        P("ep", None, None, "rep"),
        P("ep", None, "rep"),
    )
    out_specs = P(("rep", "ep"), None)
    return jax.shard_map(body, mesh=mesh, in_specs=in_specs, out_specs=out_specs, check_vma=False)
```

```python
import jax
import jax.numpy as jnp
from jax import lax
from jax.experimental import pallas as pl
from jax.experimental.pallas import tpu as pltpu
from jax.sharding import PartitionSpec as P


def slot_plan(choice_ids, expert_count, capacity):
    queue_len, picks = choice_ids.shape
    flat_ids = choice_ids.reshape(queue_len * picks)
    position = jnp.arange(queue_len * picks, dtype=jnp.int32)
    earlier = (flat_ids[:, None] == flat_ids[None, :]) & (position[None, :] < position[:, None])
    slot_rank = jnp.sum(earlier.astype(jnp.int32), axis=1)
    target = flat_ids * capacity + slot_rank
    columns = jnp.arange(expert_count * capacity, dtype=jnp.int32)
    onehot = target[:, None] == columns[None, :]
    return onehot.reshape(queue_len, picks, expert_count * capacity)


def dispatch_rows(onehot, tokens):
    placing = jnp.sum(onehot.astype(jnp.bfloat16), axis=1)
    return jnp.dot(placing.T, tokens, preferred_element_type=jnp.float32).astype(jnp.bfloat16)


def to_owners(outgoing):
    return lax.all_to_all(outgoing, "ep", split_axis=0, concat_axis=0, tiled=True)


def to_sources(results):
    return lax.all_to_all(results, "ep", split_axis=0, concat_axis=0, tiled=True)


def full_units(quarter):
    return lax.all_gather(quarter, "rep", axis=1, tiled=True)


MESH = pl.DeviceIdType.MESH
PAD = 128


TILE = 256


NZ = 4
PASSES = [
    [(0, 0, 0)],
    [(0, 0, 1), (1, 0, 0), (0, 1, 0)],
    [(1, 1, 0), (1, 0, 1), (2, 0, 0), (3, 0, 0)],
    [(1, 1, 1), (3, 1, 0), (3, 0, 1), (2, 0, 1)],
    [(3, 1, 1), (2, 1, 0), (2, 1, 1)],
    [(0, 1, 1)],
]


def dense_kernel(tok_ref, logit_ref, ids_ref, wgu_ref, wd_ref, out_ref,
                 rows, logit_v, ids_v, gate_w, up_w, down_w, hid, own, core_in, pair, keep, x_in,
                 part, z_in, zy_in, cross, y_in, x0_in, xy_in,
                 w_sem, near_send, line_send, far_recv, pass_recv, hid_send, hid_recv, core_send, core_recv,
                 x_send, x_recv, z_send, z_recv, zy_recv, y_send, y_recv, xy_recv):
    y = lax.axis_index("rep")
    ep = lax.axis_index("ep")
    z, x, c = ep // 4, (ep // 2) % 2, ep % 2
    oy, ox, oc = 1 - y, 1 - x, 1 - c
    q, width = tok_ref.shape
    units = gate_w.shape[1]
    cols = down_w.shape[1]
    nz, n_ep = NZ, 4 * NZ
    tiles = units // TILE

    def at(yy, zz, xx, cc):
        return (yy, zz * 4 + xx * 2 + cc)

    small = [
        pltpu.make_async_copy(logit_ref, logit_v, w_sem.at[0]),
        pltpu.make_async_copy(ids_ref, ids_v, w_sem.at[1]),
        pltpu.make_async_copy(tok_ref, rows.at[z, x, y, c, :, pl.ds(0, width)], w_sem.at[2]),
    ]
    weights = [
        pltpu.make_async_copy(wgu_ref.at[0, 0], gate_w, w_sem.at[3]),
        pltpu.make_async_copy(wgu_ref.at[0, 1], up_w, w_sem.at[4]),
        pltpu.make_async_copy(wd_ref.at[0], down_w, w_sem.at[5]),
    ]
    for w in small + weights:
        w.start()

    barrier = pltpu.get_barrier_semaphore()
    peers = [at(oy, z, x, c), at(y, z, ox, c), at(y, z, x, oc)]
    peers += [at(yy, (z + d) % nz, x, c) for yy in (y, oy) for d in range(1, nz)]
    peers += [at(oy, z, ox, c)]
    for p in peers:
        pl.semaphore_signal(barrier, inc=1, device_id=p, device_id_type=MESH)

    for w in small:
        w.wait()
    scaled = jnp.exp(logit_v[...])
    soft = scaled / jnp.sum(scaled, axis=0, keepdims=True)
    line = lax.broadcasted_iota(jnp.int32, (PAD, q), 0)
    expert, piece = line % n_ep, line // n_ep
    ids = ids_v[...]
    comb = jnp.zeros((PAD, q), jnp.float32)
    for k in range(ids.shape[0]):
        comb = comb + jnp.where(ids[k:k + 1, :] == expert, soft[k:k + 1, :], 0.0)
    hi = comb.astype(jnp.bfloat16).astype(jnp.float32)
    rest = comb - hi
    mid = rest.astype(jnp.bfloat16).astype(jnp.float32)
    low = rest - mid
    coded = jnp.where(piece == 0, hi, jnp.where(piece == 1, mid, jnp.where(piece == 2, low, 0.0)))
    rows[z, x, y, c, :, width:] = coded.T.astype(jnp.bfloat16)
    with jax.named_scope("entry"):
        pl.semaphore_wait(barrier, len(peers))

    near = jnp.minimum(z, nz - 1 - z)
    rising = z < nz - 1 - z
    order = [z]
    for k in range(1, nz):
        d = jnp.where(k <= 2 * near, (k + 1) // 2, k - near)
        side = jnp.where(rising, 1, -1)
        sign = jnp.where(k <= 2 * near, -side if k % 2 else side, side)
        order.append(z + sign * d)
    up, down = at(y, jnp.minimum(z + 1, nz - 1), x, c), at(y, jnp.maximum(z - 1, 0), x, c)

    chain = [[(z < nz - 1, up, 1), (z > 0, down, 2)], [], [(z == 1, down, 3), (z == 2, up, 3)]]
    pass_of = {chip: number for number, chips in enumerate(PASSES) for chip in chips}

    mine = (0, 0, 0)

    def place(chip):
        k, dx, dy = chip
        return order[k], (x, ox)[dx], (y, oy)[dy]

    def send(dev, chip, send_sem, recv_sem):
        block = rows.at[(*place(chip), c)]
        pltpu.make_async_remote_copy(
            src_ref=block, dst_ref=block, send_sem=send_sem, recv_sem=recv_sem,
            device_id=dev, device_id_type=MESH).start()

    def far_sem(s):
        return far_recv.at[(s[0] * 2 + s[1]) * 2 + s[2]]

    def wait_blocks(ref, send_sem=None, recv_sem=None):
        copy = pltpu.make_async_remote_copy(
            src_ref=ref, dst_ref=ref, send_sem=send_sem if recv_sem is None else recv_sem,
            recv_sem=send_sem if recv_sem is None else recv_sem,
            device_id=peers[0], device_id_type=MESH)
        if recv_sem is None:
            copy.wait_send()
        else:
            copy.wait_recv()

    def arrive(chip):
        wait_blocks(rows.at[(*place(chip), c)], recv_sem=far_sem(place(chip)))

    def blocks(count):
        return rows.reshape(8 * nz, q, width + PAD).at[pl.ds(0, count)]

    def arrive_pass(number):
        wait_blocks(blocks(len(PASSES[number])), recv_sem=pass_recv.at[number])

    def send_y(chip):
        send(peers[0], chip, near_send.at[0], far_sem(place(chip)))

    def send_x(chip):
        send(peers[1], chip, near_send.at[1], far_sem(place(chip)))

    def send_core(chip):
        send(peers[2], chip, near_send.at[2], pass_recv.at[pass_of[chip]])

    def take(chip):
        k, dx, dy = chip
        with jax.named_scope(f"fw{k}{dx}{dy}"):
            arrive(chip)
        send_core(chip)
        if (dx, dy) == (0, 1) and k < 3:
            for go, dev, sem in chain[k]:
                pl.when(go)(lambda: send(dev, chip, line_send.at[sem], far_sem(place(chip))))

    def hid_copy(chip, at_cols):
        k, dx = chip[:2]
        part_of = hid.at[y, k, dx, (y, oy)[chip[2]], :, at_cols]
        return pltpu.make_async_remote_copy(
            src_ref=part_of, dst_ref=part_of,
            send_sem=hid_send, recv_sem=hid_recv.at[k, dx],
            device_id=peers[0], device_id_type=MESH)

    def hidden_of(number, chips):
        with jax.named_scope(f"rows{number}"):
            arrive_pass(number)
        with jax.named_scope(f"hidden{number}"):
            block = jnp.concatenate([rows[(*place(chip),)].reshape(2 * q, width + PAD)[:, :width] for chip in chips], axis=0)
            for i in range(tiles):
                at_cols = pl.ds(i * TILE, TILE)
                gate = jnp.dot(block, gate_w[:, at_cols], preferred_element_type=jnp.float32)
                upper = jnp.dot(block, up_w[:, at_cols], preferred_element_type=jnp.float32)
                value = (jax.nn.silu(gate) * upper).astype(jnp.bfloat16)
                for j, chip in enumerate(chips):
                    yy = (y, oy)[chip[2]]
                    hid[y, chip[0], chip[1], yy, :, at_cols] = value[j * 2 * q:(j + 1) * 2 * q]
                    if number == 0:
                        hid_copy(chip, at_cols).start()
                        if i == 0:
                            send(at(oy, z, ox, c), mine, near_send.at[1], far_sem(place(mine)))

    def ship(chips):
        for chip in chips:
            hid_copy(chip, pl.ds(0, units)).start()

    def core_copy(k, dx):
        return pltpu.make_async_remote_copy(
            src_ref=own.at[k, dx, oc], dst_ref=core_in.at[k, dx],
            send_sem=core_send, recv_sem=core_recv.at[k, dx],
            device_id=peers[2], device_id_type=MESH)

    def push(src, dst, send_sem, recv_sem, dev):
        pltpu.make_async_remote_copy(
            src_ref=src, dst_ref=dst, send_sem=send_sem, recv_sem=recv_sem,
            device_id=dev, device_id_type=MESH).start()

    def outputs_of(*groups):
        size = 4 * q
        name = "".join(f"{k}{dx}" for k, dx in groups)
        with jax.named_scope(f"hid{name}"):
            for k, dx in groups:
                wait_blocks(hid.at[oy, k, dx], recv_sem=hid_recv.at[k, dx])
        with jax.named_scope(f"out{name}"):
            picked = lax.broadcasted_iota(jnp.int32, (size, PAD), 1)
            take = jnp.logical_and(picked % n_ep == ep, picked < 3 * n_ep)
            weights, halves = [], ([], [])
            for k, dx in groups:
                codes = rows[order[k], (x, ox)[dx]].reshape(size, width + PAD)[:, width:].astype(jnp.float32)
                weights.append(jnp.sum(jnp.where(take, codes, 0.0), axis=1, keepdims=True))
                for half in range(2):
                    halves[half].append(hid[half, k, dx].reshape(size, units))
            left, right = jnp.concatenate(halves[0], axis=0), jnp.concatenate(halves[1], axis=0)
            for i in range(cols // TILE):
                at_cols = pl.ds(i * TILE, TILE)
                total = jnp.dot(left, down_w[:units, at_cols], preferred_element_type=jnp.float32)
                total += jnp.dot(right, down_w[units:, at_cols], preferred_element_type=jnp.float32)
                total = total.astype(jnp.bfloat16).astype(jnp.float32)
                for j, (k, dx) in enumerate(groups):
                    value = (total[j * size:(j + 1) * size] * weights[j]).astype(jnp.bfloat16).reshape(2, 2, q, TILE)
                    own[k, dx, 0, :, :, at_cols] = value[:, 0]
                    own[k, dx, 1, :, :, at_cols] = value[:, 1]
        for k, dx in groups:
            core_copy(k, dx).start()

    def over_core(k, dx):
        with jax.named_scope(f"core{k}{dx}"):
            core_copy(k, dx).wait_recv()
        both = own[k, dx, c].astype(jnp.float32) + core_in[k, dx].astype(jnp.float32)
        if dx:
            pair[k] = both.astype(jnp.bfloat16)
            if k:
                push(pair.at[k], x_in.at[k], x_send, x_recv.at[k], peers[1])
            else:
                push(pair.at[0, oy], xy_in, x_send, xy_recv, at(oy, z, ox, c))
                push(pair.at[0, y], x0_in, x_send, x_recv.at[0], peers[1])
        else:
            keep[k] = both
            if k == 0:
                cross[...] = both.astype(jnp.bfloat16)
                push(cross.at[oy], y_in, y_send, y_recv, peers[0])

    def over_x(k):
        with jax.named_scope(f"x{k}"):
            wait_blocks(x_in.at[k], recv_sem=x_recv.at[k])
        part[k] = (keep[k] + x_in[k].astype(jnp.float32)).astype(jnp.bfloat16)
        push(part.at[k, oy], zy_in.at[z], z_send, zy_recv.at[z], at(oy, order[k], x, c))
        push(part.at[k, y], z_in.at[z], z_send, z_recv.at[z], at(y, order[k], x, c))

    send_y(mine)
    send_core(mine)
    for k in range(1, nz):
        send(at(y, order[k], x, c), mine, line_send.at[0], far_sem(place(mine)))
    send_x(mine)
    for w in weights[:2]:
        w.wait()
    middle = jnp.logical_or(z == 1, z == 2)

    def take_second():
        take((2, 0, 1))
        send_x((2, 0, 1))

    hidden_of(0, PASSES[0])
    take((0, 0, 1))
    take((1, 0, 0))
    send_x((1, 0, 0))
    take((0, 1, 0))
    hidden_of(1, PASSES[1])
    ship(PASSES[1])
    take((1, 0, 1))
    send_x((1, 0, 1))
    take((1, 1, 0))
    take((3, 0, 0))
    send_y((3, 0, 0))
    send_x((3, 0, 0))
    take((2, 0, 0))
    send_x((2, 0, 0))
    pl.when(middle)(take_second)
    take((0, 1, 1))
    hidden_of(2, PASSES[2])
    ship(PASSES[2])
    weights[2].wait()
    pl.when(jnp.logical_not(middle))(take_second)
    take((3, 0, 1))
    send_x((3, 0, 1))
    take((1, 1, 1))
    take((3, 1, 0))
    hidden_of(3, PASSES[3])
    ship(PASSES[3])
    hidden_of(5, PASSES[5])
    outputs_of((1, 0), (0, 0))
    take((2, 1, 0))
    take((3, 1, 1))
    take((2, 1, 1))
    hidden_of(4, PASSES[4])
    ship(PASSES[4])
    over_core(1, 0)
    over_core(0, 0)
    outputs_of((1, 1), (3, 0))
    ship(PASSES[5])
    over_core(1, 1)
    over_core(3, 0)
    outputs_of((3, 1))
    over_core(3, 1)
    outputs_of((2, 0), (2, 1))
    pl.when(z != 2)(lambda: over_x(1))
    over_core(2, 0)
    over_core(2, 1)
    over_x(3)
    outputs_of((0, 1))
    pl.when(z == 2)(lambda: over_x(1))
    over_core(0, 1)
    over_x(2)

    total, other = keep[0, y], jnp.zeros((q, cols), jnp.float32)
    for k in (1, 3):
        with jax.named_scope(f"z{k}"):
            wait_blocks(z_in.at[order[k]], recv_sem=z_recv.at[order[k]])
            wait_blocks(zy_in.at[order[k]], recv_sem=zy_recv.at[order[k]])
        total = total + z_in[order[k]].astype(jnp.float32)
        other = other + zy_in[order[k]].astype(jnp.float32)
    with jax.named_scope("near"):
        wait_blocks(y_in, recv_sem=y_recv)
        wait_blocks(x0_in, recv_sem=x_recv.at[0])
        wait_blocks(xy_in, recv_sem=xy_recv)
    total = total + x0_in[...].astype(jnp.float32)
    other = other + y_in[...].astype(jnp.float32) + xy_in[...].astype(jnp.float32)

    wait_blocks(blocks(2), send_sem=near_send.at[0])
    wait_blocks(blocks(2 * nz), send_sem=near_send.at[1])
    wait_blocks(blocks(4 * nz), send_sem=near_send.at[2])
    wait_blocks(blocks(nz - 1), send_sem=line_send.at[0])
    pl.when(z < nz - 1)(lambda: wait_blocks(blocks(1), send_sem=line_send.at[1]))
    pl.when(z > 0)(lambda: wait_blocks(blocks(1), send_sem=line_send.at[2]))
    pl.when(jnp.logical_or(z == 1, z == 2))(lambda: wait_blocks(blocks(1), send_sem=line_send.at[3]))
    wait_blocks(hid.at[y], send_sem=hid_send)
    wait_blocks(own.reshape(nz * 4, 2, q, cols).at[pl.ds(0, 2 * nz)], send_sem=core_send)
    wait_blocks(pair, send_sem=x_send)
    wait_blocks(part.at[pl.ds(1, nz - 1)], send_sem=z_send)
    wait_blocks(y_in, send_sem=y_send)
    with jax.named_scope("last"):
        wait_blocks(z_in.at[order[2]], recv_sem=z_recv.at[order[2]])
        wait_blocks(zy_in.at[order[2]], recv_sem=zy_recv.at[order[2]])
    total = total + z_in[order[2]].astype(jnp.float32)
    other = other + zy_in[order[2]].astype(jnp.float32)
    out_ref[:, pl.ds(pl.multiple_of(y * cols, cols), cols)] = total.astype(jnp.bfloat16)
    out_ref[:, pl.ds(pl.multiple_of(oy * cols, cols), cols)] = other.astype(jnp.bfloat16)


def dense_body(tokens, logits, expert_ids, w_gate_up, w_down):
    nz = NZ
    q, width = tokens.shape
    picks = logits.shape[1]
    units = w_gate_up.shape[3]
    cols = w_down.shape[2]
    bf, sem = jnp.bfloat16, pltpu.SemaphoreType.DMA
    vmem = pl.BlockSpec(memory_space=pltpu.VMEM)
    hbm = pl.BlockSpec(memory_space=pl.ANY)
    return pl.pallas_call(
        dense_kernel,
        out_shape=pltpu.VMEM((q, width), bf),
        in_specs=[hbm] * 5,
        out_specs=vmem,
        scratch_shapes=[
            pltpu.VMEM((nz, 2, 2, 2, q, width + PAD), bf),
            pltpu.VMEM((picks, q), jnp.float32),
            pltpu.VMEM((picks, q), jnp.int32),
            pltpu.VMEM((width, units), bf),
            pltpu.VMEM((width, units), bf),
            pltpu.VMEM((2 * units, cols), bf),
            pltpu.VMEM((2, nz, 2, 2, 2 * q, units), bf),
            pltpu.VMEM((nz, 2, 2, 2, q, cols), bf),
            pltpu.VMEM((nz, 2, 2, q, cols), bf),
            pltpu.VMEM((nz, 2, q, cols), bf),
            pltpu.VMEM((nz, 2, q, cols), jnp.float32),
            pltpu.VMEM((nz, 2, q, cols), bf),
            pltpu.VMEM((nz, 2, q, cols), bf),
            pltpu.VMEM((nz, q, cols), bf),
            pltpu.VMEM((nz, q, cols), bf),
            pltpu.VMEM((2, q, cols), bf),
            pltpu.VMEM((q, cols), bf),
            pltpu.VMEM((q, cols), bf),
            pltpu.VMEM((q, cols), bf),
            sem((6,)),
            sem((3,)), sem((4,)), sem((4 * nz,)), sem((len(PASSES),)),
            sem, sem((nz, 2)),
            sem, sem((nz, 2)),
            sem, sem((nz,)),
            sem, sem((nz,)), sem((nz,)),
            sem, sem, sem,
        ],
        compiler_params=pltpu.CompilerParams(
            collective_id=0, has_side_effects=True, vmem_limit_bytes=58 * 1024 * 1024
        ),
    )(tokens, logits.T, expert_ids.T, w_gate_up, w_down)


def body(tokens, logits, expert_ids, w_gate_up, w_down):
    expert_count = lax.axis_size("ep")
    queue_len, picks = expert_ids.shape
    features = tokens.shape[1]
    capacity = max(2, min(queue_len, 2 * queue_len * picks // expert_count))
    if capacity == queue_len and lax.axis_size("rep") == 2 and expert_count == 4 * NZ:
        return dense_body(tokens, logits, expert_ids, w_gate_up, w_down)
    slot_total = expert_count * capacity
    onehot = slot_plan(expert_ids, expert_count, capacity)
    scaled = jnp.exp(logits)
    weights = scaled / jnp.sum(scaled, axis=1, keepdims=True)
    combine = jnp.sum(weights[:, :, None] * onehot.astype(jnp.float32), axis=1)
    gate_weight = w_gate_up[0, 0]
    up_weight = w_gate_up[0, 1]
    down_weight = w_down[0]
    received = to_owners(dispatch_rows(onehot, tokens).reshape(expert_count, capacity, features))
    slot_rows = received.reshape(slot_total, features)
    portion = lax.all_gather(slot_rows, "rep", axis=0, tiled=True)
    gate_part = jnp.dot(portion, gate_weight, preferred_element_type=jnp.float32)
    upper = jnp.dot(portion, up_weight, preferred_element_type=jnp.float32)
    quarter = (jax.nn.silu(gate_part) * upper).astype(jnp.bfloat16)
    hidden = full_units(quarter)
    partial_out = jnp.dot(hidden, down_weight, preferred_element_type=jnp.float32).astype(
        jnp.bfloat16
    )
    own_rows = lax.all_to_all(partial_out, "rep", split_axis=0, concat_axis=1, tiled=True)
    returned = to_sources(own_rows.reshape(expert_count, capacity, features))
    values = returned.reshape(slot_total, features)
    mixed = jnp.dot(combine, values.astype(jnp.float32), precision=lax.Precision.HIGHEST)
    return mixed.astype(jnp.bfloat16)


def solution(mesh):
    in_specs = (
        P(("rep", "ep"), None),
        P(("rep", "ep"), None),
        P(("rep", "ep"), None),
        P("ep", None, None, "rep"),
        P("ep", None, "rep"),
    )
    out_specs = P(("rep", "ep"), None)
    return jax.shard_map(body, mesh=mesh, in_specs=in_specs, out_specs=out_specs, check_vma=False)
```

```python
import jax
import jax.numpy as jnp
from jax import lax
from jax.experimental import pallas as pl
from jax.experimental.pallas import tpu as pltpu
from jax.sharding import PartitionSpec as P


def slot_plan(choice_ids, expert_count, capacity):
    queue_len, picks = choice_ids.shape
    flat_ids = choice_ids.reshape(queue_len * picks)
    position = jnp.arange(queue_len * picks, dtype=jnp.int32)
    earlier = (flat_ids[:, None] == flat_ids[None, :]) & (position[None, :] < position[:, None])
    slot_rank = jnp.sum(earlier.astype(jnp.int32), axis=1)
    target = flat_ids * capacity + slot_rank
    columns = jnp.arange(expert_count * capacity, dtype=jnp.int32)
    onehot = target[:, None] == columns[None, :]
    return onehot.reshape(queue_len, picks, expert_count * capacity)


def dispatch_rows(onehot, tokens):
    placing = jnp.sum(onehot.astype(jnp.bfloat16), axis=1)
    return jnp.dot(placing.T, tokens, preferred_element_type=jnp.float32).astype(jnp.bfloat16)


def to_owners(outgoing):
    return lax.all_to_all(outgoing, "ep", split_axis=0, concat_axis=0, tiled=True)


def to_sources(results):
    return lax.all_to_all(results, "ep", split_axis=0, concat_axis=0, tiled=True)


def full_units(quarter):
    return lax.all_gather(quarter, "rep", axis=1, tiled=True)


MESH = pl.DeviceIdType.MESH
PAD = 128


TILE = 256


NZ = 4
PASSES = [
    [(0, 0, 0)],
    [(0, 0, 1), (1, 0, 0), (0, 1, 0)],
    [(1, 1, 0), (1, 0, 1), (2, 0, 0), (3, 0, 0)],
    [(1, 1, 1), (3, 1, 0), (3, 0, 1), (2, 0, 1)],
    [(3, 1, 1), (2, 1, 0), (2, 1, 1)],
    [(0, 1, 1)],
]


def dense_kernel(tok_ref, logit_ref, ids_ref, wgu_ref, wd_ref, out_ref,
                 rows, logit_v, ids_v, gate_w, up_w, down_w, hid, own, core_in, pair, keep, x_in,
                 part, z_in, zy_in, cross, y_in, x0_in, xy_in,
                 w_sem, near_send, line_send, far_recv, pass_recv, hid_send, hid_recv, core_send, core_recv,
                 x_send, x_recv, z_send, z_recv, zy_recv, y_send, y_recv, xy_recv):
    y = lax.axis_index("rep")
    ep = lax.axis_index("ep")
    z, x, c = ep // 4, (ep // 2) % 2, ep % 2
    oy, ox, oc = 1 - y, 1 - x, 1 - c
    q, width = tok_ref.shape
    units = gate_w.shape[1]
    cols = down_w.shape[1]
    nz, n_ep = NZ, 4 * NZ
    tiles = units // TILE

    def at(yy, zz, xx, cc):
        return (yy, zz * 4 + xx * 2 + cc)

    small = [
        pltpu.make_async_copy(logit_ref, logit_v, w_sem.at[0]),
        pltpu.make_async_copy(ids_ref, ids_v, w_sem.at[1]),
        pltpu.make_async_copy(tok_ref, rows.at[z, x, y, c, :, pl.ds(0, width)], w_sem.at[2]),
    ]
    weights = [
        pltpu.make_async_copy(wgu_ref.at[0, 0], gate_w, w_sem.at[3]),
        pltpu.make_async_copy(wgu_ref.at[0, 1], up_w, w_sem.at[4]),
        pltpu.make_async_copy(wd_ref.at[0], down_w, w_sem.at[5]),
    ]
    for w in small + weights:
        w.start()

    barrier = pltpu.get_barrier_semaphore()
    peers = [at(oy, z, x, c), at(y, z, ox, c), at(y, z, x, oc)]
    peers += [at(yy, (z + d) % nz, x, c) for yy in (y, oy) for d in range(1, nz)]
    peers += [at(oy, z, ox, c)]
    for p in peers:
        pl.semaphore_signal(barrier, inc=1, device_id=p, device_id_type=MESH)

    for w in small:
        w.wait()
    scaled = jnp.exp(logit_v[...])
    soft = scaled / jnp.sum(scaled, axis=0, keepdims=True)
    line = lax.broadcasted_iota(jnp.int32, (PAD, q), 0)
    expert, piece = line % n_ep, line // n_ep
    ids = ids_v[...]
    comb = jnp.zeros((PAD, q), jnp.float32)
    for k in range(ids.shape[0]):
        comb = comb + jnp.where(ids[k:k + 1, :] == expert, soft[k:k + 1, :], 0.0)
    hi = comb.astype(jnp.bfloat16).astype(jnp.float32)
    rest = comb - hi
    mid = rest.astype(jnp.bfloat16).astype(jnp.float32)
    low = rest - mid
    coded = jnp.where(piece == 0, hi, jnp.where(piece == 1, mid, jnp.where(piece == 2, low, 0.0)))
    rows[z, x, y, c, :, width:] = coded.T.astype(jnp.bfloat16)
    with jax.named_scope("entry"):
        pl.semaphore_wait(barrier, len(peers))

    near = jnp.minimum(z, nz - 1 - z)
    rising = z < nz - 1 - z
    order = [z]
    for k in range(1, nz):
        d = jnp.where(k <= 2 * near, (k + 1) // 2, k - near)
        side = jnp.where(rising, 1, -1)
        sign = jnp.where(k <= 2 * near, -side if k % 2 else side, side)
        order.append(z + sign * d)
    up, down = at(y, jnp.minimum(z + 1, nz - 1), x, c), at(y, jnp.maximum(z - 1, 0), x, c)

    chain = [[(z < nz - 1, up, 1), (z > 0, down, 2)], [], [(z == 1, down, 3), (z == 2, up, 3)]]
    pass_of = {chip: number for number, chips in enumerate(PASSES) for chip in chips}

    mine = (0, 0, 0)

    def place(chip):
        k, dx, dy = chip
        return order[k], (x, ox)[dx], (y, oy)[dy]

    def send(dev, chip, send_sem, recv_sem):
        block = rows.at[(*place(chip), c)]
        pltpu.make_async_remote_copy(
            src_ref=block, dst_ref=block, send_sem=send_sem, recv_sem=recv_sem,
            device_id=dev, device_id_type=MESH).start()

    def far_sem(s):
        return far_recv.at[(s[0] * 2 + s[1]) * 2 + s[2]]

    def wait_blocks(ref, send_sem=None, recv_sem=None):
        copy = pltpu.make_async_remote_copy(
            src_ref=ref, dst_ref=ref, send_sem=send_sem if recv_sem is None else recv_sem,
            recv_sem=send_sem if recv_sem is None else recv_sem,
            device_id=peers[0], device_id_type=MESH)
        if recv_sem is None:
            copy.wait_send()
        else:
            copy.wait_recv()

    def arrive(chip):
        wait_blocks(rows.at[(*place(chip), c)], recv_sem=far_sem(place(chip)))

    def blocks(count):
        return rows.reshape(8 * nz, q, width + PAD).at[pl.ds(0, count)]

    def arrive_pass(number):
        wait_blocks(blocks(len(PASSES[number])), recv_sem=pass_recv.at[number])

    def send_y(chip):
        send(peers[0], chip, near_send.at[0], far_sem(place(chip)))

    def send_x(chip):
        send(peers[1], chip, near_send.at[1], far_sem(place(chip)))

    def send_core(chip):
        send(peers[2], chip, near_send.at[2], pass_recv.at[pass_of[chip]])

    def take(chip):
        k, dx, dy = chip
        with jax.named_scope(f"fw{k}{dx}{dy}"):
            arrive(chip)
        send_core(chip)
        if (dx, dy) == (0, 1) and k < 3:
            for go, dev, sem in chain[k]:
                pl.when(go)(lambda: send(dev, chip, line_send.at[sem], far_sem(place(chip))))

    def hid_copy(chip, at_cols):
        k, dx = chip[:2]
        part_of = hid.at[y, k, dx, (y, oy)[chip[2]], :, at_cols]
        return pltpu.make_async_remote_copy(
            src_ref=part_of, dst_ref=part_of,
            send_sem=hid_send, recv_sem=hid_recv.at[k, dx],
            device_id=peers[0], device_id_type=MESH)

    def hidden_of(number, chips):
        with jax.named_scope(f"rows{number}"):
            arrive_pass(number)
        with jax.named_scope(f"hidden{number}"):
            block = jnp.concatenate([rows[(*place(chip),)].reshape(2 * q, width + PAD)[:, :width] for chip in chips], axis=0)
            for i in range(tiles):
                at_cols = pl.ds(i * TILE, TILE)
                gate = jnp.dot(block, gate_w[:, at_cols], preferred_element_type=jnp.float32)
                upper = jnp.dot(block, up_w[:, at_cols], preferred_element_type=jnp.float32)
                value = (jax.nn.silu(gate) * upper).astype(jnp.bfloat16)
                for j, chip in enumerate(chips):
                    yy = (y, oy)[chip[2]]
                    hid[y, chip[0], chip[1], yy, :, at_cols] = value[j * 2 * q:(j + 1) * 2 * q]
                    if number == 0:
                        hid_copy(chip, at_cols).start()
                        if i == 0:
                            send(at(oy, z, ox, c), mine, near_send.at[1], far_sem(place(mine)))

    def ship(chips):
        for chip in chips:
            hid_copy(chip, pl.ds(0, units)).start()

    def core_copy(k, dx):
        return pltpu.make_async_remote_copy(
            src_ref=own.at[k, dx, oc], dst_ref=core_in.at[k, dx],
            send_sem=core_send, recv_sem=core_recv.at[k, dx],
            device_id=peers[2], device_id_type=MESH)

    def push(src, dst, send_sem, recv_sem, dev):
        pltpu.make_async_remote_copy(
            src_ref=src, dst_ref=dst, send_sem=send_sem, recv_sem=recv_sem,
            device_id=dev, device_id_type=MESH).start()

    def outputs_of(*groups):
        size = 4 * q
        name = "".join(f"{k}{dx}" for k, dx in groups)
        with jax.named_scope(f"hid{name}"):
            for k, dx in groups:
                wait_blocks(hid.at[oy, k, dx], recv_sem=hid_recv.at[k, dx])
        with jax.named_scope(f"out{name}"):
            picked = lax.broadcasted_iota(jnp.int32, (size, PAD), 1)
            take = jnp.logical_and(picked % n_ep == ep, picked < 3 * n_ep)
            weights, halves = [], ([], [])
            for k, dx in groups:
                codes = rows[order[k], (x, ox)[dx]].reshape(size, width + PAD)[:, width:].astype(jnp.float32)
                weights.append(jnp.sum(jnp.where(take, codes, 0.0), axis=1, keepdims=True))
                for half in range(2):
                    halves[half].append(hid[half, k, dx].reshape(size, units))
            left, right = jnp.concatenate(halves[0], axis=0), jnp.concatenate(halves[1], axis=0)
            for i in range(cols // TILE):
                at_cols = pl.ds(i * TILE, TILE)
                total = jnp.dot(left, down_w[:units, at_cols], preferred_element_type=jnp.float32)
                total += jnp.dot(right, down_w[units:, at_cols], preferred_element_type=jnp.float32)
                total = total.astype(jnp.bfloat16).astype(jnp.float32)
                for j, (k, dx) in enumerate(groups):
                    value = (total[j * size:(j + 1) * size] * weights[j]).astype(jnp.bfloat16).reshape(2, 2, q, TILE)
                    own[k, dx, 0, :, :, at_cols] = value[:, 0]
                    own[k, dx, 1, :, :, at_cols] = value[:, 1]
        for k, dx in groups:
            core_copy(k, dx).start()

    def over_core(k, dx):
        with jax.named_scope(f"core{k}{dx}"):
            core_copy(k, dx).wait_recv()
        both = own[k, dx, c].astype(jnp.float32) + core_in[k, dx].astype(jnp.float32)
        if dx:
            pair[k] = both.astype(jnp.bfloat16)
            if k:
                push(pair.at[k], x_in.at[k], x_send, x_recv.at[k], peers[1])
            else:
                push(pair.at[0, oy], xy_in, x_send, xy_recv, at(oy, z, ox, c))
                push(pair.at[0, y], x0_in, x_send, x_recv.at[0], peers[1])
        else:
            keep[k] = both
            if k == 0:
                cross[...] = both.astype(jnp.bfloat16)
                push(cross.at[oy], y_in, y_send, y_recv, peers[0])

    def over_x(k):
        with jax.named_scope(f"x{k}"):
            wait_blocks(x_in.at[k], recv_sem=x_recv.at[k])
        part[k] = (keep[k] + x_in[k].astype(jnp.float32)).astype(jnp.bfloat16)
        push(part.at[k, oy], zy_in.at[z], z_send, zy_recv.at[z], at(oy, order[k], x, c))
        push(part.at[k, y], z_in.at[z], z_send, z_recv.at[z], at(y, order[k], x, c))

    send_y(mine)
    send_core(mine)
    for k in range(1, nz):
        send(at(y, order[k], x, c), mine, line_send.at[0], far_sem(place(mine)))
    send_x(mine)
    for w in weights[:2]:
        w.wait()
    middle = jnp.logical_or(z == 1, z == 2)

    def take_second():
        take((2, 0, 1))
        send_x((2, 0, 1))

    hidden_of(0, PASSES[0])
    take((0, 0, 1))
    take((1, 0, 0))
    send_x((1, 0, 0))
    take((0, 1, 0))
    hidden_of(1, PASSES[1])
    ship(PASSES[1])
    take((1, 0, 1))
    send_x((1, 0, 1))
    take((1, 1, 0))
    take((3, 0, 0))
    send_y((3, 0, 0))
    send_x((3, 0, 0))
    take((2, 0, 0))
    pl.when(middle)(lambda: take((2, 0, 1)))
    take((0, 1, 1))
    hidden_of(2, PASSES[2])
    ship(PASSES[2])
    send_x((2, 0, 0))
    pl.when(middle)(lambda: send_x((2, 0, 1)))
    weights[2].wait()
    pl.when(jnp.logical_not(middle))(take_second)
    take((3, 0, 1))
    send_x((3, 0, 1))
    take((1, 1, 1))
    take((3, 1, 0))
    hidden_of(3, PASSES[3])
    ship(PASSES[3])
    hidden_of(5, PASSES[5])
    outputs_of((1, 0), (0, 0))
    take((2, 1, 0))
    take((3, 1, 1))
    take((2, 1, 1))
    hidden_of(4, PASSES[4])
    ship(PASSES[4])
    over_core(1, 0)
    over_core(0, 0)
    outputs_of((1, 1), (3, 0))
    ship(PASSES[5])
    over_core(1, 1)
    over_core(3, 0)
    outputs_of((3, 1))
    over_core(3, 1)
    outputs_of((2, 0), (2, 1))
    pl.when(z != 2)(lambda: over_x(1))
    over_core(2, 0)
    over_core(2, 1)
    over_x(3)
    outputs_of((0, 1))
    pl.when(z == 2)(lambda: over_x(1))
    over_core(0, 1)
    over_x(2)

    total, other = keep[0, y], jnp.zeros((q, cols), jnp.float32)
    for k in (1, 3):
        with jax.named_scope(f"z{k}"):
            wait_blocks(z_in.at[order[k]], recv_sem=z_recv.at[order[k]])
            wait_blocks(zy_in.at[order[k]], recv_sem=zy_recv.at[order[k]])
        total = total + z_in[order[k]].astype(jnp.float32)
        other = other + zy_in[order[k]].astype(jnp.float32)
    with jax.named_scope("near"):
        wait_blocks(y_in, recv_sem=y_recv)
        wait_blocks(x0_in, recv_sem=x_recv.at[0])
        wait_blocks(xy_in, recv_sem=xy_recv)
    total = total + x0_in[...].astype(jnp.float32)
    other = other + y_in[...].astype(jnp.float32) + xy_in[...].astype(jnp.float32)

    wait_blocks(blocks(2), send_sem=near_send.at[0])
    wait_blocks(blocks(2 * nz), send_sem=near_send.at[1])
    wait_blocks(blocks(4 * nz), send_sem=near_send.at[2])
    wait_blocks(blocks(nz - 1), send_sem=line_send.at[0])
    pl.when(z < nz - 1)(lambda: wait_blocks(blocks(1), send_sem=line_send.at[1]))
    pl.when(z > 0)(lambda: wait_blocks(blocks(1), send_sem=line_send.at[2]))
    pl.when(jnp.logical_or(z == 1, z == 2))(lambda: wait_blocks(blocks(1), send_sem=line_send.at[3]))
    wait_blocks(hid.at[y], send_sem=hid_send)
    wait_blocks(own.reshape(nz * 4, 2, q, cols).at[pl.ds(0, 2 * nz)], send_sem=core_send)
    wait_blocks(pair, send_sem=x_send)
    wait_blocks(part.at[pl.ds(1, nz - 1)], send_sem=z_send)
    wait_blocks(y_in, send_sem=y_send)
    with jax.named_scope("last"):
        wait_blocks(z_in.at[order[2]], recv_sem=z_recv.at[order[2]])
        wait_blocks(zy_in.at[order[2]], recv_sem=zy_recv.at[order[2]])
    total = total + z_in[order[2]].astype(jnp.float32)
    other = other + zy_in[order[2]].astype(jnp.float32)
    out_ref[:, pl.ds(pl.multiple_of(y * cols, cols), cols)] = total.astype(jnp.bfloat16)
    out_ref[:, pl.ds(pl.multiple_of(oy * cols, cols), cols)] = other.astype(jnp.bfloat16)


def dense_body(tokens, logits, expert_ids, w_gate_up, w_down):
    nz = NZ
    q, width = tokens.shape
    picks = logits.shape[1]
    units = w_gate_up.shape[3]
    cols = w_down.shape[2]
    bf, sem = jnp.bfloat16, pltpu.SemaphoreType.DMA
    vmem = pl.BlockSpec(memory_space=pltpu.VMEM)
    hbm = pl.BlockSpec(memory_space=pl.ANY)
    return pl.pallas_call(
        dense_kernel,
        out_shape=pltpu.VMEM((q, width), bf),
        in_specs=[hbm] * 5,
        out_specs=vmem,
        scratch_shapes=[
            pltpu.VMEM((nz, 2, 2, 2, q, width + PAD), bf),
            pltpu.VMEM((picks, q), jnp.float32),
            pltpu.VMEM((picks, q), jnp.int32),
            pltpu.VMEM((width, units), bf),
            pltpu.VMEM((width, units), bf),
            pltpu.VMEM((2 * units, cols), bf),
            pltpu.VMEM((2, nz, 2, 2, 2 * q, units), bf),
            pltpu.VMEM((nz, 2, 2, 2, q, cols), bf),
            pltpu.VMEM((nz, 2, 2, q, cols), bf),
            pltpu.VMEM((nz, 2, q, cols), bf),
            pltpu.VMEM((nz, 2, q, cols), jnp.float32),
            pltpu.VMEM((nz, 2, q, cols), bf),
            pltpu.VMEM((nz, 2, q, cols), bf),
            pltpu.VMEM((nz, q, cols), bf),
            pltpu.VMEM((nz, q, cols), bf),
            pltpu.VMEM((2, q, cols), bf),
            pltpu.VMEM((q, cols), bf),
            pltpu.VMEM((q, cols), bf),
            pltpu.VMEM((q, cols), bf),
            sem((6,)),
            sem((3,)), sem((4,)), sem((4 * nz,)), sem((len(PASSES),)),
            sem, sem((nz, 2)),
            sem, sem((nz, 2)),
            sem, sem((nz,)),
            sem, sem((nz,)), sem((nz,)),
            sem, sem, sem,
        ],
        compiler_params=pltpu.CompilerParams(
            collective_id=0, has_side_effects=True, vmem_limit_bytes=58 * 1024 * 1024
        ),
    )(tokens, logits.T, expert_ids.T, w_gate_up, w_down)


def body(tokens, logits, expert_ids, w_gate_up, w_down):
    expert_count = lax.axis_size("ep")
    queue_len, picks = expert_ids.shape
    features = tokens.shape[1]
    capacity = max(2, min(queue_len, 2 * queue_len * picks // expert_count))
    if capacity == queue_len and lax.axis_size("rep") == 2 and expert_count == 4 * NZ:
        return dense_body(tokens, logits, expert_ids, w_gate_up, w_down)
    slot_total = expert_count * capacity
    onehot = slot_plan(expert_ids, expert_count, capacity)
    scaled = jnp.exp(logits)
    weights = scaled / jnp.sum(scaled, axis=1, keepdims=True)
    combine = jnp.sum(weights[:, :, None] * onehot.astype(jnp.float32), axis=1)
    gate_weight = w_gate_up[0, 0]
    up_weight = w_gate_up[0, 1]
    down_weight = w_down[0]
    received = to_owners(dispatch_rows(onehot, tokens).reshape(expert_count, capacity, features))
    slot_rows = received.reshape(slot_total, features)
    portion = lax.all_gather(slot_rows, "rep", axis=0, tiled=True)
    gate_part = jnp.dot(portion, gate_weight, preferred_element_type=jnp.float32)
    upper = jnp.dot(portion, up_weight, preferred_element_type=jnp.float32)
    quarter = (jax.nn.silu(gate_part) * upper).astype(jnp.bfloat16)
    hidden = full_units(quarter)
    partial_out = jnp.dot(hidden, down_weight, preferred_element_type=jnp.float32).astype(
        jnp.bfloat16
    )
    own_rows = lax.all_to_all(partial_out, "rep", split_axis=0, concat_axis=1, tiled=True)
    returned = to_sources(own_rows.reshape(expert_count, capacity, features))
    values = returned.reshape(slot_total, features)
    mixed = jnp.dot(combine, values.astype(jnp.float32), precision=lax.Precision.HIGHEST)
    return mixed.astype(jnp.bfloat16)


def solution(mesh):
    in_specs = (
        P(("rep", "ep"), None),
        P(("rep", "ep"), None),
        P(("rep", "ep"), None),
        P("ep", None, None, "rep"),
        P("ep", None, "rep"),
    )
    out_specs = P(("rep", "ep"), None)
    return jax.shard_map(body, mesh=mesh, in_specs=in_specs, out_specs=out_specs, check_vma=False)
```

```python
import jax
import jax.numpy as jnp
from jax import lax
from jax.experimental import pallas as pl
from jax.experimental.pallas import tpu as pltpu
from jax.sharding import PartitionSpec as P


def slot_plan(choice_ids, expert_count, capacity):
    queue_len, picks = choice_ids.shape
    flat_ids = choice_ids.reshape(queue_len * picks)
    position = jnp.arange(queue_len * picks, dtype=jnp.int32)
    earlier = (flat_ids[:, None] == flat_ids[None, :]) & (position[None, :] < position[:, None])
    slot_rank = jnp.sum(earlier.astype(jnp.int32), axis=1)
    target = flat_ids * capacity + slot_rank
    columns = jnp.arange(expert_count * capacity, dtype=jnp.int32)
    onehot = target[:, None] == columns[None, :]
    return onehot.reshape(queue_len, picks, expert_count * capacity)


def dispatch_rows(onehot, tokens):
    placing = jnp.sum(onehot.astype(jnp.bfloat16), axis=1)
    return jnp.dot(placing.T, tokens, preferred_element_type=jnp.float32).astype(jnp.bfloat16)


def to_owners(outgoing):
    return lax.all_to_all(outgoing, "ep", split_axis=0, concat_axis=0, tiled=True)


def to_sources(results):
    return lax.all_to_all(results, "ep", split_axis=0, concat_axis=0, tiled=True)


def full_units(quarter):
    return lax.all_gather(quarter, "rep", axis=1, tiled=True)


MESH = pl.DeviceIdType.MESH
PAD = 128


TILE = 256


NZ = 4
PASSES = [
    [(0, 0, 0)],
    [(0, 0, 1), (1, 0, 0), (0, 1, 0)],
    [(1, 1, 0), (1, 0, 1), (2, 0, 0), (3, 0, 0)],
    [(1, 1, 1), (3, 1, 0), (3, 0, 1), (2, 0, 1)],
    [(3, 1, 1), (2, 1, 0), (2, 1, 1)],
    [(0, 1, 1)],
]


def dense_kernel(tok_ref, logit_ref, ids_ref, wgu_ref, wd_ref, out_ref,
                 rows, logit_v, ids_v, gate_w, up_w, down_w, hid, own, core_in, pair, keep, x_in,
                 part, z_in, zy_in, cross, y_in, x0_in, xy_in,
                 w_sem, near_send, line_send, far_recv, pass_recv, hid_send, hid_recv, core_send, core_recv,
                 x_send, x_recv, z_send, z_recv, zy_recv, y_send, y_recv, xy_recv):
    y = lax.axis_index("rep")
    ep = lax.axis_index("ep")
    z, x, c = ep // 4, (ep // 2) % 2, ep % 2
    oy, ox, oc = 1 - y, 1 - x, 1 - c
    q, width = tok_ref.shape
    units = gate_w.shape[1]
    cols = down_w.shape[1]
    nz, n_ep = NZ, 4 * NZ
    tiles = units // TILE

    def at(yy, zz, xx, cc):
        return (yy, zz * 4 + xx * 2 + cc)

    small = [
        pltpu.make_async_copy(logit_ref, logit_v, w_sem.at[0]),
        pltpu.make_async_copy(ids_ref, ids_v, w_sem.at[1]),
        pltpu.make_async_copy(tok_ref, rows.at[z, x, y, c, :, pl.ds(0, width)], w_sem.at[2]),
    ]
    weights = [
        pltpu.make_async_copy(wgu_ref.at[0, 0], gate_w, w_sem.at[3]),
        pltpu.make_async_copy(wgu_ref.at[0, 1], up_w, w_sem.at[4]),
        pltpu.make_async_copy(wd_ref.at[0], down_w, w_sem.at[5]),
    ]
    for w in small + weights:
        w.start()

    barrier = pltpu.get_barrier_semaphore()
    peers = [at(oy, z, x, c), at(y, z, ox, c), at(y, z, x, oc)]
    peers += [at(yy, (z + d) % nz, x, c) for yy in (y, oy) for d in range(1, nz)]
    peers += [at(oy, z, ox, c)]
    for p in peers:
        pl.semaphore_signal(barrier, inc=1, device_id=p, device_id_type=MESH)

    for w in small:
        w.wait()
    scaled = jnp.exp(logit_v[...])
    soft = scaled / jnp.sum(scaled, axis=0, keepdims=True)
    line = lax.broadcasted_iota(jnp.int32, (PAD, q), 0)
    expert, piece = line % n_ep, line // n_ep
    ids = ids_v[...]
    comb = jnp.zeros((PAD, q), jnp.float32)
    for k in range(ids.shape[0]):
        comb = comb + jnp.where(ids[k:k + 1, :] == expert, soft[k:k + 1, :], 0.0)
    hi = comb.astype(jnp.bfloat16).astype(jnp.float32)
    rest = comb - hi
    mid = rest.astype(jnp.bfloat16).astype(jnp.float32)
    low = rest - mid
    coded = jnp.where(piece == 0, hi, jnp.where(piece == 1, mid, jnp.where(piece == 2, low, 0.0)))
    rows[z, x, y, c, :, width:] = coded.T.astype(jnp.bfloat16)
    with jax.named_scope("entry"):
        pl.semaphore_wait(barrier, len(peers))

    near = jnp.minimum(z, nz - 1 - z)
    rising = z < nz - 1 - z
    order = [z]
    for k in range(1, nz):
        d = jnp.where(k <= 2 * near, (k + 1) // 2, k - near)
        side = jnp.where(rising, 1, -1)
        sign = jnp.where(k <= 2 * near, -side if k % 2 else side, side)
        order.append(z + sign * d)
    up, down = at(y, jnp.minimum(z + 1, nz - 1), x, c), at(y, jnp.maximum(z - 1, 0), x, c)

    chain = [[(z < nz - 1, up, 1), (z > 0, down, 2)], [], [(z == 1, down, 3), (z == 2, up, 3)]]
    pass_of = {chip: number for number, chips in enumerate(PASSES) for chip in chips}

    mine = (0, 0, 0)

    def place(chip):
        k, dx, dy = chip
        return order[k], (x, ox)[dx], (y, oy)[dy]

    def send(dev, chip, send_sem, recv_sem):
        block = rows.at[(*place(chip), c)]
        pltpu.make_async_remote_copy(
            src_ref=block, dst_ref=block, send_sem=send_sem, recv_sem=recv_sem,
            device_id=dev, device_id_type=MESH).start()

    def far_sem(s):
        return far_recv.at[(s[0] * 2 + s[1]) * 2 + s[2]]

    def wait_blocks(ref, send_sem=None, recv_sem=None):
        copy = pltpu.make_async_remote_copy(
            src_ref=ref, dst_ref=ref, send_sem=send_sem if recv_sem is None else recv_sem,
            recv_sem=send_sem if recv_sem is None else recv_sem,
            device_id=peers[0], device_id_type=MESH)
        if recv_sem is None:
            copy.wait_send()
        else:
            copy.wait_recv()

    def arrive(chip):
        wait_blocks(rows.at[(*place(chip), c)], recv_sem=far_sem(place(chip)))

    def blocks(count):
        return rows.reshape(8 * nz, q, width + PAD).at[pl.ds(0, count)]

    def arrive_pass(number):
        wait_blocks(blocks(len(PASSES[number])), recv_sem=pass_recv.at[number])

    def send_y(chip):
        send(peers[0], chip, near_send.at[0], far_sem(place(chip)))

    def send_x(chip):
        send(peers[1], chip, near_send.at[1], far_sem(place(chip)))

    def send_core(chip):
        send(peers[2], chip, near_send.at[2], pass_recv.at[pass_of[chip]])

    def take(chip):
        k, dx, dy = chip
        with jax.named_scope(f"fw{k}{dx}{dy}"):
            arrive(chip)
        send_core(chip)
        if (dx, dy) == (0, 1) and k < 3:
            for go, dev, sem in chain[k]:
                pl.when(go)(lambda: send(dev, chip, line_send.at[sem], far_sem(place(chip))))

    def hid_copy(chip, at_cols):
        k, dx = chip[:2]
        part_of = hid.at[y, k, dx, (y, oy)[chip[2]], :, at_cols]
        return pltpu.make_async_remote_copy(
            src_ref=part_of, dst_ref=part_of,
            send_sem=hid_send, recv_sem=hid_recv.at[k, dx],
            device_id=peers[0], device_id_type=MESH)

    def hidden_of(number, chips):
        with jax.named_scope(f"rows{number}"):
            arrive_pass(number)
        with jax.named_scope(f"hidden{number}"):
            block = jnp.concatenate([rows[(*place(chip),)].reshape(2 * q, width + PAD)[:, :width] for chip in chips], axis=0)
            for i in range(tiles):
                at_cols = pl.ds(i * TILE, TILE)
                gate = jnp.dot(block, gate_w[:, at_cols], preferred_element_type=jnp.float32)
                upper = jnp.dot(block, up_w[:, at_cols], preferred_element_type=jnp.float32)
                value = (jax.nn.silu(gate) * upper).astype(jnp.bfloat16)
                for j, chip in enumerate(chips):
                    yy = (y, oy)[chip[2]]
                    hid[y, chip[0], chip[1], yy, :, at_cols] = value[j * 2 * q:(j + 1) * 2 * q]
                    if number == 0:
                        hid_copy(chip, at_cols).start()
                        if i == 0:
                            send(at(oy, z, ox, c), mine, near_send.at[1], far_sem(place(mine)))

    def ship(chips):
        for chip in chips:
            hid_copy(chip, pl.ds(0, units)).start()

    def core_copy(k, dx):
        return pltpu.make_async_remote_copy(
            src_ref=own.at[k, dx, oc], dst_ref=core_in.at[k, dx],
            send_sem=core_send, recv_sem=core_recv.at[k, dx],
            device_id=peers[2], device_id_type=MESH)

    def push(src, dst, send_sem, recv_sem, dev):
        pltpu.make_async_remote_copy(
            src_ref=src, dst_ref=dst, send_sem=send_sem, recv_sem=recv_sem,
            device_id=dev, device_id_type=MESH).start()

    def outputs_of(*groups):
        size = 4 * q
        name = "".join(f"{k}{dx}" for k, dx in groups)
        with jax.named_scope(f"hid{name}"):
            for k, dx in groups:
                wait_blocks(hid.at[oy, k, dx], recv_sem=hid_recv.at[k, dx])
        with jax.named_scope(f"out{name}"):
            picked = lax.broadcasted_iota(jnp.int32, (size, PAD), 1)
            take = jnp.logical_and(picked % n_ep == ep, picked < 3 * n_ep)
            weights, halves = [], ([], [])
            for k, dx in groups:
                codes = rows[order[k], (x, ox)[dx]].reshape(size, width + PAD)[:, width:].astype(jnp.float32)
                weights.append(jnp.sum(jnp.where(take, codes, 0.0), axis=1, keepdims=True))
                for half in range(2):
                    halves[half].append(hid[half, k, dx].reshape(size, units))
            left, right = jnp.concatenate(halves[0], axis=0), jnp.concatenate(halves[1], axis=0)
            for i in range(cols // TILE):
                at_cols = pl.ds(i * TILE, TILE)
                total = jnp.dot(left, down_w[:units, at_cols], preferred_element_type=jnp.float32)
                total += jnp.dot(right, down_w[units:, at_cols], preferred_element_type=jnp.float32)
                total = total.astype(jnp.bfloat16).astype(jnp.float32)
                for j, (k, dx) in enumerate(groups):
                    value = (total[j * size:(j + 1) * size] * weights[j]).astype(jnp.bfloat16).reshape(2, 2, q, TILE)
                    own[k, dx, 0, :, :, at_cols] = value[:, 0]
                    own[k, dx, 1, :, :, at_cols] = value[:, 1]
        for k, dx in groups:
            core_copy(k, dx).start()

    def over_core(k, dx):
        with jax.named_scope(f"core{k}{dx}"):
            core_copy(k, dx).wait_recv()
        both = own[k, dx, c].astype(jnp.float32) + core_in[k, dx].astype(jnp.float32)
        if dx:
            pair[k] = both.astype(jnp.bfloat16)
            if k:
                push(pair.at[k], x_in.at[k], x_send, x_recv.at[k], peers[1])
            else:
                push(pair.at[0, oy], xy_in, x_send, xy_recv, at(oy, z, ox, c))
                push(pair.at[0, y], x0_in, x_send, x_recv.at[0], peers[1])
        else:
            keep[k] = both
            if k == 0:
                cross[...] = both.astype(jnp.bfloat16)
                push(cross.at[oy], y_in, y_send, y_recv, peers[0])

    def over_x(k):
        with jax.named_scope(f"x{k}"):
            wait_blocks(x_in.at[k], recv_sem=x_recv.at[k])
        part[k] = (keep[k] + x_in[k].astype(jnp.float32)).astype(jnp.bfloat16)
        push(part.at[k, oy], zy_in.at[z], z_send, zy_recv.at[z], at(oy, order[k], x, c))
        push(part.at[k, y], z_in.at[z], z_send, z_recv.at[z], at(y, order[k], x, c))

    send_y(mine)
    send_core(mine)
    for k in range(1, nz):
        send(at(y, order[k], x, c), mine, line_send.at[0], far_sem(place(mine)))
    send_x(mine)
    for w in weights[:2]:
        w.wait()
    middle = jnp.logical_or(z == 1, z == 2)

    def take_second():
        take((2, 0, 1))
        send_x((2, 0, 1))

    hidden_of(0, PASSES[0])
    take((0, 0, 1))
    take((1, 0, 0))
    send_x((1, 0, 0))
    take((0, 1, 0))
    hidden_of(1, PASSES[1])
    ship(PASSES[1])
    take((1, 0, 1))
    send_x((1, 0, 1))
    take((1, 1, 0))
    take((3, 0, 0))
    send_y((3, 0, 0))
    send_x((3, 0, 0))
    take((2, 0, 0))
    pl.when(middle)(lambda: take((2, 0, 1)))
    take((0, 1, 1))
    hidden_of(2, PASSES[2])
    ship(PASSES[2])
    send_x((2, 0, 0))
    pl.when(middle)(lambda: send_x((2, 0, 1)))
    weights[2].wait()
    pl.when(jnp.logical_not(middle))(take_second)
    take((3, 0, 1))
    send_x((3, 0, 1))
    take((1, 1, 1))
    take((3, 1, 0))
    hidden_of(3, PASSES[3])
    ship(PASSES[3])
    hidden_of(5, PASSES[5])
    outputs_of((1, 0), (0, 0))
    take((2, 1, 0))
    take((3, 1, 1))
    take((2, 1, 1))
    hidden_of(4, PASSES[4])
    ship(PASSES[4])
    over_core(1, 0)
    over_core(0, 0)
    outputs_of((1, 1), (3, 0))
    ship(PASSES[5])
    over_core(1, 1)
    outputs_of((3, 1))
    over_core(3, 1)
    over_core(3, 0)
    outputs_of((2, 0), (2, 1))
    pl.when(z != 2)(lambda: over_x(1))
    over_core(2, 0)
    over_core(2, 1)
    over_x(3)
    outputs_of((0, 1))
    pl.when(z == 2)(lambda: over_x(1))
    over_core(0, 1)
    over_x(2)

    total, other = keep[0, y], jnp.zeros((q, cols), jnp.float32)
    for k in (1, 3):
        with jax.named_scope(f"z{k}"):
            wait_blocks(z_in.at[order[k]], recv_sem=z_recv.at[order[k]])
            wait_blocks(zy_in.at[order[k]], recv_sem=zy_recv.at[order[k]])
        total = total + z_in[order[k]].astype(jnp.float32)
        other = other + zy_in[order[k]].astype(jnp.float32)
    with jax.named_scope("near"):
        wait_blocks(y_in, recv_sem=y_recv)
        wait_blocks(x0_in, recv_sem=x_recv.at[0])
        wait_blocks(xy_in, recv_sem=xy_recv)
    total = total + x0_in[...].astype(jnp.float32)
    other = other + y_in[...].astype(jnp.float32) + xy_in[...].astype(jnp.float32)

    wait_blocks(blocks(2), send_sem=near_send.at[0])
    wait_blocks(blocks(2 * nz), send_sem=near_send.at[1])
    wait_blocks(blocks(4 * nz), send_sem=near_send.at[2])
    wait_blocks(blocks(nz - 1), send_sem=line_send.at[0])
    pl.when(z < nz - 1)(lambda: wait_blocks(blocks(1), send_sem=line_send.at[1]))
    pl.when(z > 0)(lambda: wait_blocks(blocks(1), send_sem=line_send.at[2]))
    pl.when(jnp.logical_or(z == 1, z == 2))(lambda: wait_blocks(blocks(1), send_sem=line_send.at[3]))
    wait_blocks(hid.at[y], send_sem=hid_send)
    wait_blocks(own.reshape(nz * 4, 2, q, cols).at[pl.ds(0, 2 * nz)], send_sem=core_send)
    wait_blocks(pair, send_sem=x_send)
    wait_blocks(part.at[pl.ds(1, nz - 1)], send_sem=z_send)
    wait_blocks(y_in, send_sem=y_send)
    with jax.named_scope("last"):
        wait_blocks(z_in.at[order[2]], recv_sem=z_recv.at[order[2]])
        wait_blocks(zy_in.at[order[2]], recv_sem=zy_recv.at[order[2]])
    total = total + z_in[order[2]].astype(jnp.float32)
    other = other + zy_in[order[2]].astype(jnp.float32)
    out_ref[:, pl.ds(pl.multiple_of(y * cols, cols), cols)] = total.astype(jnp.bfloat16)
    out_ref[:, pl.ds(pl.multiple_of(oy * cols, cols), cols)] = other.astype(jnp.bfloat16)


def dense_body(tokens, logits, expert_ids, w_gate_up, w_down):
    nz = NZ
    q, width = tokens.shape
    picks = logits.shape[1]
    units = w_gate_up.shape[3]
    cols = w_down.shape[2]
    bf, sem = jnp.bfloat16, pltpu.SemaphoreType.DMA
    vmem = pl.BlockSpec(memory_space=pltpu.VMEM)
    hbm = pl.BlockSpec(memory_space=pl.ANY)
    return pl.pallas_call(
        dense_kernel,
        out_shape=pltpu.VMEM((q, width), bf),
        in_specs=[hbm] * 5,
        out_specs=vmem,
        scratch_shapes=[
            pltpu.VMEM((nz, 2, 2, 2, q, width + PAD), bf),
            pltpu.VMEM((picks, q), jnp.float32),
            pltpu.VMEM((picks, q), jnp.int32),
            pltpu.VMEM((width, units), bf),
            pltpu.VMEM((width, units), bf),
            pltpu.VMEM((2 * units, cols), bf),
            pltpu.VMEM((2, nz, 2, 2, 2 * q, units), bf),
            pltpu.VMEM((nz, 2, 2, 2, q, cols), bf),
            pltpu.VMEM((nz, 2, 2, q, cols), bf),
            pltpu.VMEM((nz, 2, q, cols), bf),
            pltpu.VMEM((nz, 2, q, cols), jnp.float32),
            pltpu.VMEM((nz, 2, q, cols), bf),
            pltpu.VMEM((nz, 2, q, cols), bf),
            pltpu.VMEM((nz, q, cols), bf),
            pltpu.VMEM((nz, q, cols), bf),
            pltpu.VMEM((2, q, cols), bf),
            pltpu.VMEM((q, cols), bf),
            pltpu.VMEM((q, cols), bf),
            pltpu.VMEM((q, cols), bf),
            sem((6,)),
            sem((3,)), sem((4,)), sem((4 * nz,)), sem((len(PASSES),)),
            sem, sem((nz, 2)),
            sem, sem((nz, 2)),
            sem, sem((nz,)),
            sem, sem((nz,)), sem((nz,)),
            sem, sem, sem,
        ],
        compiler_params=pltpu.CompilerParams(
            collective_id=0, has_side_effects=True, vmem_limit_bytes=58 * 1024 * 1024
        ),
    )(tokens, logits.T, expert_ids.T, w_gate_up, w_down)


def body(tokens, logits, expert_ids, w_gate_up, w_down):
    expert_count = lax.axis_size("ep")
    queue_len, picks = expert_ids.shape
    features = tokens.shape[1]
    capacity = max(2, min(queue_len, 2 * queue_len * picks // expert_count))
    if capacity == queue_len and lax.axis_size("rep") == 2 and expert_count == 4 * NZ:
        return dense_body(tokens, logits, expert_ids, w_gate_up, w_down)
    slot_total = expert_count * capacity
    onehot = slot_plan(expert_ids, expert_count, capacity)
    scaled = jnp.exp(logits)
    weights = scaled / jnp.sum(scaled, axis=1, keepdims=True)
    combine = jnp.sum(weights[:, :, None] * onehot.astype(jnp.float32), axis=1)
    gate_weight = w_gate_up[0, 0]
    up_weight = w_gate_up[0, 1]
    down_weight = w_down[0]
    received = to_owners(dispatch_rows(onehot, tokens).reshape(expert_count, capacity, features))
    slot_rows = received.reshape(slot_total, features)
    portion = lax.all_gather(slot_rows, "rep", axis=0, tiled=True)
    gate_part = jnp.dot(portion, gate_weight, preferred_element_type=jnp.float32)
    upper = jnp.dot(portion, up_weight, preferred_element_type=jnp.float32)
    quarter = (jax.nn.silu(gate_part) * upper).astype(jnp.bfloat16)
    hidden = full_units(quarter)
    partial_out = jnp.dot(hidden, down_weight, preferred_element_type=jnp.float32).astype(
        jnp.bfloat16
    )
    own_rows = lax.all_to_all(partial_out, "rep", split_axis=0, concat_axis=1, tiled=True)
    returned = to_sources(own_rows.reshape(expert_count, capacity, features))
    values = returned.reshape(slot_total, features)
    mixed = jnp.dot(combine, values.astype(jnp.float32), precision=lax.Precision.HIGHEST)
    return mixed.astype(jnp.bfloat16)


def solution(mesh):
    in_specs = (
        P(("rep", "ep"), None),
        P(("rep", "ep"), None),
        P(("rep", "ep"), None),
        P("ep", None, None, "rep"),
        P("ep", None, "rep"),
    )
    out_specs = P(("rep", "ep"), None)
    return jax.shard_map(body, mesh=mesh, in_specs=in_specs, out_specs=out_specs, check_vma=False)
```

```python
import jax
import jax.numpy as jnp
from jax import lax
from jax.experimental import pallas as pl
from jax.experimental.pallas import tpu as pltpu
from jax.sharding import PartitionSpec as P


def slot_plan(choice_ids, expert_count, capacity):
    queue_len, picks = choice_ids.shape
    flat_ids = choice_ids.reshape(queue_len * picks)
    position = jnp.arange(queue_len * picks, dtype=jnp.int32)
    earlier = (flat_ids[:, None] == flat_ids[None, :]) & (position[None, :] < position[:, None])
    slot_rank = jnp.sum(earlier.astype(jnp.int32), axis=1)
    target = flat_ids * capacity + slot_rank
    columns = jnp.arange(expert_count * capacity, dtype=jnp.int32)
    onehot = target[:, None] == columns[None, :]
    return onehot.reshape(queue_len, picks, expert_count * capacity)


def dispatch_rows(onehot, tokens):
    placing = jnp.sum(onehot.astype(jnp.bfloat16), axis=1)
    return jnp.dot(placing.T, tokens, preferred_element_type=jnp.float32).astype(jnp.bfloat16)


def to_owners(outgoing):
    return lax.all_to_all(outgoing, "ep", split_axis=0, concat_axis=0, tiled=True)


def to_sources(results):
    return lax.all_to_all(results, "ep", split_axis=0, concat_axis=0, tiled=True)


def full_units(quarter):
    return lax.all_gather(quarter, "rep", axis=1, tiled=True)


MESH = pl.DeviceIdType.MESH
PAD = 128


TILE = 256


NZ = 4
PASSES = [
    [(0, 0, 0)],
    [(0, 0, 1), (1, 0, 0), (0, 1, 0)],
    [(1, 1, 0), (1, 0, 1), (2, 0, 0), (3, 0, 0)],
    [(1, 1, 1), (3, 1, 0), (3, 0, 1), (2, 0, 1)],
    [(3, 1, 1), (2, 1, 0), (2, 1, 1)],
    [(0, 1, 1)],
]


def dense_kernel(tok_ref, logit_ref, ids_ref, wgu_ref, wd_ref, out_ref,
                 rows, logit_v, ids_v, gate_w, up_w, down_w, hid, own, core_in, pair, keep, x_in,
                 part, z_in, zy_in, cross, y_in, x0_in, xy_in,
                 w_sem, near_send, line_send, far_recv, pass_recv, hid_send, hid_recv, core_send, core_recv,
                 x_send, x_recv, z_send, z_recv, zy_recv, y_send, y_recv, xy_recv):
    y = lax.axis_index("rep")
    ep = lax.axis_index("ep")
    z, x, c = ep // 4, (ep // 2) % 2, ep % 2
    oy, ox, oc = 1 - y, 1 - x, 1 - c
    q, width = tok_ref.shape
    units = gate_w.shape[1]
    cols = down_w.shape[1]
    nz, n_ep = NZ, 4 * NZ
    tiles = units // TILE

    def at(yy, zz, xx, cc):
        return (yy, zz * 4 + xx * 2 + cc)

    small = [
        pltpu.make_async_copy(logit_ref, logit_v, w_sem.at[0]),
        pltpu.make_async_copy(ids_ref, ids_v, w_sem.at[1]),
        pltpu.make_async_copy(tok_ref, rows.at[z, x, y, c, :, pl.ds(0, width)], w_sem.at[2]),
    ]
    weights = [
        pltpu.make_async_copy(wgu_ref.at[0, 0], gate_w, w_sem.at[3]),
        pltpu.make_async_copy(wgu_ref.at[0, 1], up_w, w_sem.at[4]),
        pltpu.make_async_copy(wd_ref.at[0], down_w, w_sem.at[5]),
    ]
    for w in small + weights:
        w.start()

    barrier = pltpu.get_barrier_semaphore()
    peers = [at(oy, z, x, c), at(y, z, ox, c), at(y, z, x, oc)]
    peers += [at(yy, (z + d) % nz, x, c) for yy in (y, oy) for d in range(1, nz)]
    peers += [at(oy, z, ox, c)]
    for p in peers:
        pl.semaphore_signal(barrier, inc=1, device_id=p, device_id_type=MESH)

    for w in small:
        w.wait()
    scaled = jnp.exp(logit_v[...])
    soft = scaled / jnp.sum(scaled, axis=0, keepdims=True)
    line = lax.broadcasted_iota(jnp.int32, (PAD, q), 0)
    expert, piece = line % n_ep, line // n_ep
    ids = ids_v[...]
    comb = jnp.zeros((PAD, q), jnp.float32)
    for k in range(ids.shape[0]):
        comb = comb + jnp.where(ids[k:k + 1, :] == expert, soft[k:k + 1, :], 0.0)
    hi = comb.astype(jnp.bfloat16).astype(jnp.float32)
    rest = comb - hi
    mid = rest.astype(jnp.bfloat16).astype(jnp.float32)
    low = rest - mid
    coded = jnp.where(piece == 0, hi, jnp.where(piece == 1, mid, jnp.where(piece == 2, low, 0.0)))
    rows[z, x, y, c, :, width:] = coded.T.astype(jnp.bfloat16)
    with jax.named_scope("entry"):
        pl.semaphore_wait(barrier, len(peers))

    near = jnp.minimum(z, nz - 1 - z)
    rising = z < nz - 1 - z
    order = [z]
    for k in range(1, nz):
        d = jnp.where(k <= 2 * near, (k + 1) // 2, k - near)
        side = jnp.where(rising, 1, -1)
        sign = jnp.where(k <= 2 * near, -side if k % 2 else side, side)
        order.append(z + sign * d)
    up, down = at(y, jnp.minimum(z + 1, nz - 1), x, c), at(y, jnp.maximum(z - 1, 0), x, c)

    chain = [[(z < nz - 1, up, 1), (z > 0, down, 2)], [], [(z == 1, down, 3), (z == 2, up, 3)]]
    pass_of = {chip: number for number, chips in enumerate(PASSES) for chip in chips}

    mine = (0, 0, 0)

    def place(chip):
        k, dx, dy = chip
        return order[k], (x, ox)[dx], (y, oy)[dy]

    def send(dev, chip, send_sem, recv_sem):
        block = rows.at[(*place(chip), c)]
        pltpu.make_async_remote_copy(
            src_ref=block, dst_ref=block, send_sem=send_sem, recv_sem=recv_sem,
            device_id=dev, device_id_type=MESH).start()

    def far_sem(s):
        return far_recv.at[(s[0] * 2 + s[1]) * 2 + s[2]]

    def wait_blocks(ref, send_sem=None, recv_sem=None):
        copy = pltpu.make_async_remote_copy(
            src_ref=ref, dst_ref=ref, send_sem=send_sem if recv_sem is None else recv_sem,
            recv_sem=send_sem if recv_sem is None else recv_sem,
            device_id=peers[0], device_id_type=MESH)
        if recv_sem is None:
            copy.wait_send()
        else:
            copy.wait_recv()

    def arrive(chip):
        wait_blocks(rows.at[(*place(chip), c)], recv_sem=far_sem(place(chip)))

    def blocks(count):
        return rows.reshape(8 * nz, q, width + PAD).at[pl.ds(0, count)]

    def arrive_pass(number):
        wait_blocks(blocks(len(PASSES[number])), recv_sem=pass_recv.at[number])

    def send_y(chip):
        send(peers[0], chip, near_send.at[0], far_sem(place(chip)))

    def send_x(chip):
        send(peers[1], chip, near_send.at[1], far_sem(place(chip)))

    def send_core(chip):
        send(peers[2], chip, near_send.at[2], pass_recv.at[pass_of[chip]])

    def take(chip):
        k, dx, dy = chip
        with jax.named_scope(f"fw{k}{dx}{dy}"):
            arrive(chip)
        send_core(chip)
        if (dx, dy) == (0, 1) and k < 3:
            for go, dev, sem in chain[k]:
                pl.when(go)(lambda: send(dev, chip, line_send.at[sem], far_sem(place(chip))))

    def hid_copy(chip, at_cols):
        k, dx = chip[:2]
        part_of = hid.at[y, k, dx, (y, oy)[chip[2]], :, at_cols]
        return pltpu.make_async_remote_copy(
            src_ref=part_of, dst_ref=part_of,
            send_sem=hid_send, recv_sem=hid_recv.at[k, dx],
            device_id=peers[0], device_id_type=MESH)

    def hidden_of(number, chips):
        with jax.named_scope(f"rows{number}"):
            arrive_pass(number)
        with jax.named_scope(f"hidden{number}"):
            block = jnp.concatenate([rows[(*place(chip),)].reshape(2 * q, width + PAD)[:, :width] for chip in chips], axis=0)
            for i in range(tiles):
                at_cols = pl.ds(i * TILE, TILE)
                gate = jnp.dot(block, gate_w[:, at_cols], preferred_element_type=jnp.float32)
                upper = jnp.dot(block, up_w[:, at_cols], preferred_element_type=jnp.float32)
                value = (jax.nn.silu(gate) * upper).astype(jnp.bfloat16)
                for j, chip in enumerate(chips):
                    yy = (y, oy)[chip[2]]
                    hid[y, chip[0], chip[1], yy, :, at_cols] = value[j * 2 * q:(j + 1) * 2 * q]
                    if number == 0:
                        hid_copy(chip, at_cols).start()
                        if i == 0:
                            send(at(oy, z, ox, c), mine, near_send.at[1], far_sem(place(mine)))

    def ship(chips):
        for chip in chips:
            hid_copy(chip, pl.ds(0, units)).start()

    def core_copy(k, dx):
        return pltpu.make_async_remote_copy(
            src_ref=own.at[k, dx, oc], dst_ref=core_in.at[k, dx],
            send_sem=core_send, recv_sem=core_recv.at[k, dx],
            device_id=peers[2], device_id_type=MESH)

    def push(src, dst, send_sem, recv_sem, dev):
        pltpu.make_async_remote_copy(
            src_ref=src, dst_ref=dst, send_sem=send_sem, recv_sem=recv_sem,
            device_id=dev, device_id_type=MESH).start()

    def outputs_of(*groups):
        size = 4 * q
        name = "".join(f"{k}{dx}" for k, dx in groups)
        with jax.named_scope(f"hid{name}"):
            for k, dx in groups:
                wait_blocks(hid.at[oy, k, dx], recv_sem=hid_recv.at[k, dx])
        with jax.named_scope(f"out{name}"):
            picked = lax.broadcasted_iota(jnp.int32, (size, PAD), 1)
            take = jnp.logical_and(picked % n_ep == ep, picked < 3 * n_ep)
            weights, halves = [], ([], [])
            for k, dx in groups:
                codes = rows[order[k], (x, ox)[dx]].reshape(size, width + PAD)[:, width:].astype(jnp.float32)
                weights.append(jnp.sum(jnp.where(take, codes, 0.0), axis=1, keepdims=True))
                for half in range(2):
                    halves[half].append(hid[half, k, dx].reshape(size, units))
            left, right = jnp.concatenate(halves[0], axis=0), jnp.concatenate(halves[1], axis=0)
            for i in range(cols // TILE):
                at_cols = pl.ds(i * TILE, TILE)
                total = jnp.dot(left, down_w[:units, at_cols], preferred_element_type=jnp.float32)
                total += jnp.dot(right, down_w[units:, at_cols], preferred_element_type=jnp.float32)
                total = total.astype(jnp.bfloat16).astype(jnp.float32)
                for j, (k, dx) in enumerate(groups):
                    value = (total[j * size:(j + 1) * size] * weights[j]).astype(jnp.bfloat16).reshape(2, 2, q, TILE)
                    own[k, dx, 0, :, :, at_cols] = value[:, 0]
                    own[k, dx, 1, :, :, at_cols] = value[:, 1]
        for k, dx in groups:
            core_copy(k, dx).start()

    def over_core(k, dx):
        with jax.named_scope(f"core{k}{dx}"):
            core_copy(k, dx).wait_recv()
        both = own[k, dx, c].astype(jnp.float32) + core_in[k, dx].astype(jnp.float32)
        if dx:
            pair[k] = both.astype(jnp.bfloat16)
            if k:
                push(pair.at[k], x_in.at[k], x_send, x_recv.at[k], peers[1])
            else:
                push(pair.at[0, oy], xy_in, x_send, xy_recv, at(oy, z, ox, c))
                push(pair.at[0, y], x0_in, x_send, x_recv.at[0], peers[1])
        else:
            keep[k] = both
            if k == 0:
                cross[...] = both.astype(jnp.bfloat16)
                push(cross.at[oy], y_in, y_send, y_recv, peers[0])

    def over_x(k):
        with jax.named_scope(f"x{k}"):
            wait_blocks(x_in.at[k], recv_sem=x_recv.at[k])
        part[k] = (keep[k] + x_in[k].astype(jnp.float32)).astype(jnp.bfloat16)
        push(part.at[k, oy], zy_in.at[z], z_send, zy_recv.at[z], at(oy, order[k], x, c))
        push(part.at[k, y], z_in.at[z], z_send, z_recv.at[z], at(y, order[k], x, c))

    send_y(mine)
    send_core(mine)
    for k in range(1, nz):
        send(at(y, order[k], x, c), mine, line_send.at[0], far_sem(place(mine)))
    send_x(mine)
    for w in weights[:2]:
        w.wait()
    middle = jnp.logical_or(z == 1, z == 2)

    def take_second():
        take((2, 0, 1))
        send_x((2, 0, 1))

    hidden_of(0, PASSES[0])
    take((0, 0, 1))
    take((1, 0, 0))
    send_x((1, 0, 0))
    take((0, 1, 0))
    hidden_of(1, PASSES[1])
    ship(PASSES[1])
    take((1, 0, 1))
    take((1, 1, 0))
    take((3, 0, 0))
    send_y((3, 0, 0))
    send_x((3, 0, 0))
    send_x((1, 0, 1))
    take((2, 0, 0))
    pl.when(middle)(lambda: take((2, 0, 1)))
    take((0, 1, 1))
    hidden_of(2, PASSES[2])
    ship(PASSES[2])
    send_x((2, 0, 0))
    pl.when(middle)(lambda: send_x((2, 0, 1)))
    weights[2].wait()
    pl.when(jnp.logical_not(middle))(take_second)
    take((3, 0, 1))
    send_x((3, 0, 1))
    take((1, 1, 1))
    take((3, 1, 0))
    hidden_of(3, PASSES[3])
    ship(PASSES[3])
    hidden_of(5, PASSES[5])
    outputs_of((1, 0), (0, 0))
    take((2, 1, 0))
    take((3, 1, 1))
    take((2, 1, 1))
    hidden_of(4, PASSES[4])
    ship(PASSES[4])
    over_core(1, 0)
    over_core(0, 0)
    outputs_of((1, 1), (3, 0))
    ship(PASSES[5])
    over_core(1, 1)
    over_core(3, 0)
    outputs_of((3, 1))
    over_core(3, 1)
    outputs_of((2, 0), (2, 1))
    pl.when(z != 2)(lambda: over_x(1))
    over_core(2, 0)
    over_core(2, 1)
    over_x(3)
    outputs_of((0, 1))
    pl.when(z == 2)(lambda: over_x(1))
    over_core(0, 1)
    over_x(2)

    total, other = keep[0, y], jnp.zeros((q, cols), jnp.float32)
    for k in (1, 3):
        with jax.named_scope(f"z{k}"):
            wait_blocks(z_in.at[order[k]], recv_sem=z_recv.at[order[k]])
            wait_blocks(zy_in.at[order[k]], recv_sem=zy_recv.at[order[k]])
        total = total + z_in[order[k]].astype(jnp.float32)
        other = other + zy_in[order[k]].astype(jnp.float32)
    with jax.named_scope("near"):
        wait_blocks(y_in, recv_sem=y_recv)
        wait_blocks(x0_in, recv_sem=x_recv.at[0])
        wait_blocks(xy_in, recv_sem=xy_recv)
    total = total + x0_in[...].astype(jnp.float32)
    other = other + y_in[...].astype(jnp.float32) + xy_in[...].astype(jnp.float32)

    wait_blocks(blocks(2), send_sem=near_send.at[0])
    wait_blocks(blocks(2 * nz), send_sem=near_send.at[1])
    wait_blocks(blocks(4 * nz), send_sem=near_send.at[2])
    wait_blocks(blocks(nz - 1), send_sem=line_send.at[0])
    pl.when(z < nz - 1)(lambda: wait_blocks(blocks(1), send_sem=line_send.at[1]))
    pl.when(z > 0)(lambda: wait_blocks(blocks(1), send_sem=line_send.at[2]))
    pl.when(jnp.logical_or(z == 1, z == 2))(lambda: wait_blocks(blocks(1), send_sem=line_send.at[3]))
    wait_blocks(hid.at[y], send_sem=hid_send)
    wait_blocks(own.reshape(nz * 4, 2, q, cols).at[pl.ds(0, 2 * nz)], send_sem=core_send)
    wait_blocks(pair, send_sem=x_send)
    wait_blocks(part.at[pl.ds(1, nz - 1)], send_sem=z_send)
    wait_blocks(y_in, send_sem=y_send)
    with jax.named_scope("last"):
        wait_blocks(z_in.at[order[2]], recv_sem=z_recv.at[order[2]])
        wait_blocks(zy_in.at[order[2]], recv_sem=zy_recv.at[order[2]])
    total = total + z_in[order[2]].astype(jnp.float32)
    other = other + zy_in[order[2]].astype(jnp.float32)
    out_ref[:, pl.ds(pl.multiple_of(y * cols, cols), cols)] = total.astype(jnp.bfloat16)
    out_ref[:, pl.ds(pl.multiple_of(oy * cols, cols), cols)] = other.astype(jnp.bfloat16)


def dense_body(tokens, logits, expert_ids, w_gate_up, w_down):
    nz = NZ
    q, width = tokens.shape
    picks = logits.shape[1]
    units = w_gate_up.shape[3]
    cols = w_down.shape[2]
    bf, sem = jnp.bfloat16, pltpu.SemaphoreType.DMA
    vmem = pl.BlockSpec(memory_space=pltpu.VMEM)
    hbm = pl.BlockSpec(memory_space=pl.ANY)
    return pl.pallas_call(
        dense_kernel,
        out_shape=pltpu.VMEM((q, width), bf),
        in_specs=[hbm] * 5,
        out_specs=vmem,
        scratch_shapes=[
            pltpu.VMEM((nz, 2, 2, 2, q, width + PAD), bf),
            pltpu.VMEM((picks, q), jnp.float32),
            pltpu.VMEM((picks, q), jnp.int32),
            pltpu.VMEM((width, units), bf),
            pltpu.VMEM((width, units), bf),
            pltpu.VMEM((2 * units, cols), bf),
            pltpu.VMEM((2, nz, 2, 2, 2 * q, units), bf),
            pltpu.VMEM((nz, 2, 2, 2, q, cols), bf),
            pltpu.VMEM((nz, 2, 2, q, cols), bf),
            pltpu.VMEM((nz, 2, q, cols), bf),
            pltpu.VMEM((nz, 2, q, cols), jnp.float32),
            pltpu.VMEM((nz, 2, q, cols), bf),
            pltpu.VMEM((nz, 2, q, cols), bf),
            pltpu.VMEM((nz, q, cols), bf),
            pltpu.VMEM((nz, q, cols), bf),
            pltpu.VMEM((2, q, cols), bf),
            pltpu.VMEM((q, cols), bf),
            pltpu.VMEM((q, cols), bf),
            pltpu.VMEM((q, cols), bf),
            sem((6,)),
            sem((3,)), sem((4,)), sem((4 * nz,)), sem((len(PASSES),)),
            sem, sem((nz, 2)),
            sem, sem((nz, 2)),
            sem, sem((nz,)),
            sem, sem((nz,)), sem((nz,)),
            sem, sem, sem,
        ],
        compiler_params=pltpu.CompilerParams(
            collective_id=0, has_side_effects=True, vmem_limit_bytes=58 * 1024 * 1024
        ),
    )(tokens, logits.T, expert_ids.T, w_gate_up, w_down)


def body(tokens, logits, expert_ids, w_gate_up, w_down):
    expert_count = lax.axis_size("ep")
    queue_len, picks = expert_ids.shape
    features = tokens.shape[1]
    capacity = max(2, min(queue_len, 2 * queue_len * picks // expert_count))
    if capacity == queue_len and lax.axis_size("rep") == 2 and expert_count == 4 * NZ:
        return dense_body(tokens, logits, expert_ids, w_gate_up, w_down)
    slot_total = expert_count * capacity
    onehot = slot_plan(expert_ids, expert_count, capacity)
    scaled = jnp.exp(logits)
    weights = scaled / jnp.sum(scaled, axis=1, keepdims=True)
    combine = jnp.sum(weights[:, :, None] * onehot.astype(jnp.float32), axis=1)
    gate_weight = w_gate_up[0, 0]
    up_weight = w_gate_up[0, 1]
    down_weight = w_down[0]
    received = to_owners(dispatch_rows(onehot, tokens).reshape(expert_count, capacity, features))
    slot_rows = received.reshape(slot_total, features)
    portion = lax.all_gather(slot_rows, "rep", axis=0, tiled=True)
    gate_part = jnp.dot(portion, gate_weight, preferred_element_type=jnp.float32)
    upper = jnp.dot(portion, up_weight, preferred_element_type=jnp.float32)
    quarter = (jax.nn.silu(gate_part) * upper).astype(jnp.bfloat16)
    hidden = full_units(quarter)
    partial_out = jnp.dot(hidden, down_weight, preferred_element_type=jnp.float32).astype(
        jnp.bfloat16
    )
    own_rows = lax.all_to_all(partial_out, "rep", split_axis=0, concat_axis=1, tiled=True)
    returned = to_sources(own_rows.reshape(expert_count, capacity, features))
    values = returned.reshape(slot_total, features)
    mixed = jnp.dot(combine, values.astype(jnp.float32), precision=lax.Precision.HIGHEST)
    return mixed.astype(jnp.bfloat16)


def solution(mesh):
    in_specs = (
        P(("rep", "ep"), None),
        P(("rep", "ep"), None),
        P(("rep", "ep"), None),
        P("ep", None, None, "rep"),
        P("ep", None, "rep"),
    )
    out_specs = P(("rep", "ep"), None)
    return jax.shard_map(body, mesh=mesh, in_specs=in_specs, out_specs=out_specs, check_vma=False)
```
